32 devices in a mesh: seq: 8 (over z, y), tp: 4 (over x, core).
Axes of the slice: x: 2, y: 2, z: 4, core: 2. Of those that a mesh axis runs over, the one named last changes fastest.
Arguments:
- tokens: bfloat16 [8192, 1152], P('seq', 'tp'), may hold values from -6 to 6
- out_grad: bfloat16 [8192, 1152], P('seq', 'tp'), may hold values from -6 to 6
- route_mask: int32 [8192], P('seq'), may hold values from 0 to 1, as said below
- kept_counts: int32 [32], replicated, may hold values from 64 to 192, as said below
- labels: int32 [32], replicated, may hold values from 0 to 1000
- timesteps: int32 [32], replicated, may hold values from 0 to 999
- class_table: bfloat16 [1001, 1152], replicated, may hold values from -6 to 6
- ada_weight: bfloat16 [1152, 6, 1152], P(None, None, 'tp'), may hold values from -0.1875 to 0.1875
- ada_bias: bfloat16 [6, 1152], P(None, 'tp'), may hold values from -2 to 2
- qkv_weight: bfloat16 [1152, 3, 1152], P(None, None, 'tp'), may hold values from -0.1875 to 0.1875
- qv_bias: bfloat16 [2, 1152], P(None, 'tp'), may hold values from -2 to 2
- proj_weight: bfloat16 [1152, 1152], P('tp'), may hold values from -0.5 to 0.5
- proj_bias: bfloat16 [1152], P('tp'), may hold values from -2 to 2
- hidden_weight: bfloat16 [1152, 4608], P(None, 'tp'), may hold values from -0.1875 to 0.1875
- hidden_bias: bfloat16 [4608], P('tp'), may hold values from -2 to 2
- output_weight: bfloat16 [4608, 1152], P('tp'), may hold values from -0.09375 to 0.09375
- output_bias: bfloat16 [1152], P('tp'), may hold values from -2 to 2
Outputs:
- output: bfloat16 [8192, 1152], P('seq', 'tp')
- tokens_grad: bfloat16 [8192, 1152], P('seq', 'tp')
- class_grad: float32 [1001, 1152], P(None, 'seq')
- ada_weight_grad: float32 [1152, 6, 1152], P('seq', None, 'tp')
- ada_bias_grad: float32 [6, 1152], P(None, 'tp')
- qkv_weight_grad: float32 [1152, 3, 1152], P('seq', None, 'tp')
- qv_bias_grad: float32 [2, 1152], P(None, 'tp')
- proj_weight_grad: float32 [1152, 1152], P('tp', 'seq')
- proj_bias_grad: float32 [1152], P('tp')
- hidden_weight_grad: float32 [1152, 4608], P('seq', 'tp')
- hidden_bias_grad: float32 [4608], P('tp')
- output_weight_grad: float32 [4608, 1152], P('tp', 'seq')
- output_bias_grad: float32 [1152], P('tp')
The draws below stay inside these ranges and needn't reach their ends.
Inputs may be any that keep to these rules, and one draw needn't show every extreme that they name: route_mask keeps exactly kept_counts[i] of the 256 tokens of image i. The kept tokens of all images number 512 * 8; the kept tokens of the first j * 4 images exceed j * 512 by 0 to 128 for every j, by exactly 128 for some j, and by 0 at the end. Every aligned block of 4 images has one image with 192 kept tokens. `route_mask`: consistent with kept_counts.
All inputs are finite; a program needn't handle non-finite values.
Results may differ from the reference program's by a relative error of at most 0.025.
The reference program's roundings to bfloat16 on the way count: a program that leaves them out, or rounds other values in their place, can miss the bound.
Values may be sent and summed in bfloat16 or wider, within the bound.
A program may use at most 192 MiB of HBM per device.

```python
import math
import jax
import jax.numpy as jnp
from jax import lax

D = 1152
HEADS = 16
HEAD_DIM = 72
FF = 4608
CLASSES = 1001
IMG_TOK = 256
STEPS = 1000
IMG_DEV = 4
KEEP_MOST = 192
KEEP_LEAST = 64
K_ROWS = 512
SPILL = 128
IMAGES = 32
TOKENS = 8192


def route_counts(key):
    base_key = jax.random.fold_in(key, 11)
    device_count = IMAGES // IMG_DEV
    spill_key, pick_key, noise_key, perm_key = jax.random.split(base_key, 4)
    carried = jax.random.randint(spill_key, (device_count,), 0, SPILL + 1).astype(jnp.int32)
    chosen = jax.random.randint(pick_key, (), 0, device_count - 1)
    carried = carried.at[chosen].set(SPILL).at[device_count - 1].set(0)
    carried_in = jnp.concatenate([jnp.zeros((1,), jnp.int32), carried[:-1]])
    own_total = K_ROWS + carried - carried_in
    rest_total = own_total - KEEP_MOST
    others = IMG_DEV - 1
    base_share = rest_total // others
    extra_ones = rest_total % others
    slot_ids = jnp.arange(others, dtype=jnp.int32)
    shares = base_share[:, None] + (slot_ids[None, :] < extra_ones[:, None]).astype(jnp.int32)
    noise_room = jnp.maximum(jnp.minimum(base_share - KEEP_LEAST, KEEP_MOST - 2 - base_share) // 2, 0)
    noise_draw = jax.random.randint(noise_key, (device_count, others), -noise_room[:, None], noise_room[:, None] + 1).astype(jnp.int32)
    shares = shares + noise_draw - jnp.roll(noise_draw, 1, axis=1)
    values = jnp.concatenate([jnp.full((device_count, 1), KEEP_MOST, jnp.int32), shares], axis=1)
    image_perm = jax.vmap(lambda sub_key: jax.random.permutation(sub_key, IMG_DEV))(jax.random.split(perm_key, device_count))
    return jnp.take_along_axis(values, image_perm, axis=1).reshape(IMAGES).astype(jnp.int32)


def draw_kept_counts(key, part):
    return route_counts(key)


def draw_route_mask(key, part):
    counts = route_counts(key)
    image_keys = jax.random.split(jax.random.fold_in(key, 23), IMAGES)
    token_ranks = jax.vmap(lambda sub_key: jax.random.permutation(sub_key, IMG_TOK))(image_keys)
    return (token_ranks < counts[:, None]).astype(jnp.int32).reshape(TOKENS)


def touch_ends(array, rng, smallest, top_value):
    index_at = [jax.random.randint(jax.random.fold_in(rng, axis), (), 0, length) for axis, length in enumerate(array.shape)]
    longest = array.shape.index(max(array.shape))
    neighbour = index_at[:longest] + [(index_at[longest] + 1) % array.shape[longest]] + index_at[longest + 1:]
    return array.at[tuple(index_at)].set(smallest).at[tuple(neighbour)].set(top_value)


def shard_levels(key, extent, shards, low, largest):
    def one(position, shards_of):
        draws = jax.random.uniform(jax.random.fold_in(jax.random.fold_in(key, 6), position), (shards_of,), jnp.float32, low / len(shards), largest / len(shards))
        return jnp.repeat(jnp.exp(draws), extent[position] // shards_of).reshape((-1,) + (1,) * (len(extent) - position - 1))

    level = one(*shards[0])
    for cut in shards[1:]:
        level = level * one(*cut)
    return level


def normal_values(stream_key, extent, spread, most, cuts=(), held_as=jnp.bfloat16):
    drawn = spread * jax.random.normal(stream_key, extent, jnp.float32)
    if cuts:
        drawn = drawn * shard_levels(stream_key, extent, cuts, -0.22, 0.18)
    return jnp.clip(drawn, -most, most).astype(held_as)


def setup_inputs(seed: int = 0) -> dict:
    splits = jax.random.split(jax.random.key(seed), 18)
    tokens = normal_values(splits[0], (TOKENS, D), 1.0, 6.0, ((0, 8), (1, 4)))
    out_grad = normal_values(splits[1], (TOKENS, D), 1.0, 6.0, ((0, 8), (1, 4)))
    route_mask = draw_route_mask(jax.random.fold_in(splits[17], 71), 0)
    kept_counts = draw_kept_counts(jax.random.fold_in(splits[17], 71), 0)
    labels = touch_ends(jax.random.randint(splits[4], (IMAGES,), 0, CLASSES), jax.random.fold_in(splits[4], 1), 0, CLASSES - 1).astype(jnp.int32)
    timesteps = touch_ends(jax.random.randint(splits[5], (IMAGES,), 0, STEPS), jax.random.fold_in(splits[5], 1), 0, STEPS - 1).astype(jnp.int32)
    class_table = normal_values(splits[6], (CLASSES, D), 1.0, 6.0)
    ada_weight = normal_values(splits[7], (D, 6, D), D ** -0.5, 0.1875, ((2, 4),))
    ada_bias = normal_values(splits[8], (6, D), 0.3, 2.0, ((1, 4),))
    qkv_weight = normal_values(splits[9], (D, 3, D), D ** -0.5, 0.1875, ((2, 4),))
    qv_bias = normal_values(splits[10], (2, D), 0.3, 2.0, ((1, 4),))
    proj_weight = normal_values(splits[11], (D, D), (D // 8) ** -0.5, 0.5, ((0, 4),))
    proj_bias = normal_values(splits[12], (D,), 0.3, 2.0, ((0, 4),))
    hidden_weight = normal_values(splits[13], (D, FF), D ** -0.5, 0.1875, ((1, 4),))
    hidden_bias = normal_values(splits[14], (FF,), 0.3, 2.0, ((0, 4),))
    output_weight = normal_values(splits[15], (FF, D), FF ** -0.5, 0.09375, ((0, 4),))
    output_bias = normal_values(splits[16], (D,), 0.3, 2.0, ((0, 4),))
    return {"tokens": tokens, "out_grad": out_grad, "route_mask": route_mask, "kept_counts": kept_counts, "labels": labels, "timesteps": timesteps, "class_table": class_table, "ada_weight": ada_weight, "ada_bias": ada_bias, "qkv_weight": qkv_weight, "qv_bias": qv_bias, "proj_weight": proj_weight, "proj_bias": proj_bias, "hidden_weight": hidden_weight, "hidden_bias": hidden_bias, "output_weight": output_weight, "output_bias": output_bias}


NORM_EPS = 1e-06
HIGHEST = lax.Precision.HIGHEST

@jax.custom_vjp
def low(v):
    return lax.optimization_barrier(v.astype(jnp.bfloat16)).astype(jnp.float32)

@jax.custom_vjp
def low_back(v):
    return v

def low_keep(v):
    return (low(v), None)

def low_pass(kept, grad):
    return (grad,)

def back_keep(v):
    return (v, None)

def back_low(kept, grad):
    return (low(grad),)
low.defvjp(low_keep, low_pass)
low_back.defvjp(back_keep, back_low)

def exact_dot(left_mat, right_mat):
    return jnp.dot(left_mat, right_mat, precision=HIGHEST, preferred_element_type=jnp.float32)

def time_embed(step_ids, model_width):
    half_width = model_width // 2
    frequency = jnp.exp(-math.log(10000.0) * jnp.arange(half_width, dtype=jnp.float32) / half_width)
    angles = step_ids.astype(jnp.float32)[:, None] * frequency[None, :]
    return jnp.concatenate([jnp.cos(angles), jnp.sin(angles)], axis=1)

def norm_last(values):
    centered = values - lax.optimization_barrier(jnp.mean(values, axis=-1, keepdims=True))
    return centered * lax.rsqrt(lax.optimization_barrier(jnp.mean(centered * centered, axis=-1, keepdims=True)) + NORM_EPS)

def gelu_tanh(values):
    return jax.nn.gelu(values, approximate=True)

def reference(tokens, out_grad, route_mask, kept_counts, labels, timesteps, class_table, ada_weight, ada_bias, qkv_weight, qv_bias, proj_weight, proj_bias, hidden_weight, hidden_bias, output_weight, output_bias):
    weights = tuple((item.astype(jnp.float32) for item in (class_table, ada_weight, ada_bias, qkv_weight, qv_bias, proj_weight, proj_bias, hidden_weight, hidden_bias, output_weight, output_bias)))
    tokens_f = tokens.astype(jnp.float32)
    image_masks = route_mask.reshape(IMAGES, IMG_TOK)
    order_idx = jnp.argsort(1 - image_masks, axis=1, stable=True)[:, :KEEP_MOST].astype(jnp.int32)
    token_rank = jnp.clip(jnp.cumsum(image_masks, axis=1) - 1, 0, KEEP_MOST - 1).astype(jnp.int32)
    row_valid = jnp.arange(KEEP_MOST, dtype=jnp.int32)[None, :] < kept_counts[:, None]
    time_feats = time_embed(timesteps, D)
    label_hot = (labels[:, None] == jnp.arange(CLASSES, dtype=jnp.int32)[None, :]).astype(jnp.float32)
    group = math.gcd(IMAGES, 16)
    groups = IMAGES // group
    scale_factor = HEAD_DIM ** (-0.5)

    def forward(params, tokens_in):
        emb_table, w_ada, b_ada, w_qkv, b_qv, w_proj, b_proj, w_hidden, b_hidden, w_output, b_output = params
        condition = exact_dot(label_hot, emb_table) + time_feats
        cond_low = low(jax.nn.silu(condition))
        modulation = exact_dot(cond_low, w_ada.reshape(D, 6 * D)).reshape(IMAGES, 6, D) + b_ada[None]
        b_qkv = jnp.stack([b_qv[0], jnp.zeros_like(b_qv[0]), b_qv[1]])

        def one_group(packed):
            grp_tokens, grp_order, grp_rank, grp_mask, grp_valid, grp_mod = packed
            kept = jnp.take_along_axis(grp_tokens, grp_order[:, :, None], axis=1)
            normed_one = norm_last(kept)
            branch_one = low(normed_one * (1.0 + grp_mod[:, 1][:, None]) + grp_mod[:, 0][:, None])
            qkv_rows = jnp.einsum('gkd,dcf->gkcf', branch_one, w_qkv, precision=HIGHEST) + b_qkv
            qkv_rows = low(low_back(qkv_rows))
            query = qkv_rows[:, :, 0].reshape(group, KEEP_MOST, HEADS, HEAD_DIM)
            keys_all = qkv_rows[:, :, 1].reshape(group, KEEP_MOST, HEADS, HEAD_DIM)
            vals_all = qkv_rows[:, :, 2].reshape(group, KEEP_MOST, HEADS, HEAD_DIM)
            raw = jnp.einsum('gqhe,gkhe->ghqk', query, keys_all, precision=HIGHEST) * scale_factor
            masked = low_back(jnp.where(grp_valid[:, None, None, :], raw, -1e+30))
            top_score = lax.optimization_barrier(jnp.max(masked, axis=3, keepdims=True))
            exp_scores = jnp.exp(masked - top_score)
            attn_probs = exp_scores / lax.optimization_barrier(jnp.sum(exp_scores, axis=3, keepdims=True))
            attended = jnp.einsum('ghqk,gkhe->gqhe', low(attn_probs), vals_all, precision=HIGHEST).reshape(group, KEEP_MOST, D)
            attended = low(low_back(attended))
            attn_out = low_back(jnp.einsum('gkd,de->gke', attended, w_proj, precision=HIGHEST) + b_proj)
            middle = kept + grp_mod[:, 2][:, None] * attn_out
            normed_two = norm_last(low(middle))
            branch_two = low(normed_two * (1.0 + grp_mod[:, 4][:, None]) + grp_mod[:, 3][:, None])
            pre_act = low_back(jnp.einsum('gkd,df->gkf', branch_two, w_hidden, precision=HIGHEST) + b_hidden)
            act_low = low(gelu_tanh(pre_act))
            mlp_out = low_back(jnp.einsum('gkf,fd->gkd', act_low, w_output, precision=HIGHEST) + b_output)
            result = middle + grp_mod[:, 5][:, None] * mlp_out
            placed = jnp.take_along_axis(result, grp_rank[:, :, None], axis=1)
            return jnp.where(grp_mask[:, :, None] > 0, placed, grp_tokens)
        stacked = lax.map(jax.checkpoint(one_group), (tokens_in.reshape(groups, group, IMG_TOK, D), order_idx.reshape(groups, group, KEEP_MOST), token_rank.reshape(groups, group, IMG_TOK), image_masks.reshape(groups, group, IMG_TOK), row_valid.reshape(groups, group, KEEP_MOST), modulation.reshape(groups, group, 6, D)))
        return stacked.reshape(TOKENS, D)
    result, pullback = jax.vjp(forward, weights, tokens_f)
    weight_grads, tokens_grad = pullback(out_grad.astype(jnp.float32))
    g_table, g_ada_w, g_ada_b, g_qkv_w, g_qv_b, g_proj_w, g_proj_b, g_hidden_w, g_hidden_b, g_output_w, g_output_b = weight_grads
    return (result.astype(jnp.bfloat16), tokens_grad.astype(jnp.bfloat16), g_table, g_ada_w, g_ada_b, g_qkv_w, g_qv_b, g_proj_w, g_proj_b, g_hidden_w, g_hidden_b, g_output_w, g_output_b)
```

```python
import math

import jax
import jax.numpy as jnp
from jax import lax
from jax.sharding import PartitionSpec as P

HEAD_DIM = 72
IMG_DEV = 4
ROWS = 640


NORM_EPS = 1e-06
HIGHEST = lax.Precision.HIGHEST


def exact_dot(left_mat, right_mat):
    return jnp.dot(left_mat, right_mat, precision=HIGHEST, preferred_element_type=jnp.float32)


def time_embed(step_ids, model_width):
    half_width = model_width // 2
    frequency = jnp.exp(-math.log(10000.0) * jnp.arange(half_width, dtype=jnp.float32) / half_width)
    angles = step_ids.astype(jnp.float32)[:, None] * frequency[None, :]
    return jnp.concatenate([jnp.cos(angles), jnp.sin(angles)], axis=1)


def norm_rows(values):
    centered = values - jnp.mean(values, axis=1, keepdims=True)
    inverse = lax.rsqrt(jnp.mean(centered * centered, axis=1, keepdims=True) + NORM_EPS)
    return (centered * inverse, inverse)


def gelu_tanh(values):
    return jax.nn.gelu(values, approximate=True)


def local(
    tokens,
    out_grad,
    route_mask,
    kept_counts,
    labels,
    timesteps,
    class_table,
    ada_weight,
    ada_bias,
    qkv_weight,
    qv_bias,
    proj_weight,
    proj_bias,
    hidden_weight,
    hidden_bias,
    output_weight,
    output_bias,
):
    f32, bf16 = jnp.float32, jnp.bfloat16
    seq_index = lax.axis_index("seq")
    tp_index = lax.axis_index("tp")
    seq_size = lax.axis_size("seq")
    col_local = tokens.shape[1]
    model_width = class_table.shape[1]
    head_cols = qkv_weight.shape[2]
    heads_local = head_cols // HEAD_DIM
    slice_width = model_width // seq_size
    images = kept_counts.shape[0]
    scale_factor = HEAD_DIM ** (-0.5)
    col_start = tp_index * col_local
    first_image = seq_index * IMG_DEV
    own_counts = lax.dynamic_slice_in_dim(kept_counts, first_image, IMG_DEV)
    own_ends = jnp.cumsum(own_counts)
    rank = jnp.where(route_mask > 0, jnp.cumsum(route_mask) - 1, -1)
    row_ids = jnp.arange(ROWS, dtype=jnp.int32)
    place = (rank[None, :] == row_ids[:, None]).astype(bf16)
    row_image = jnp.sum((own_ends[None, :] <= row_ids[:, None]).astype(jnp.int32), axis=1)
    row_onehot = (row_image[:, None] == jnp.arange(IMG_DEV, dtype=jnp.int32)[None, :]).astype(f32)

    def whole_rows(part_rows):
        return lax.all_gather(part_rows, "tp", axis=1, tiled=True)

    def column_sum(part_rows):
        return lax.psum_scatter(
            part_rows.astype(bf16), "tp", scatter_dimension=1, tiled=True
        ).astype(f32)

    def own_cols(full_rows):
        return lax.dynamic_slice_in_dim(full_rows, col_start, col_local, 1)

    def reinsert(rows_new, initial):
        placed = jnp.einsum("rt,rc->tc", place, rows_new, preferred_element_type=f32).astype(bf16)
        return jnp.where(route_mask[:, None] > 0, placed, initial)

    label_hot = (
        labels[:, None] == jnp.arange(class_table.shape[0], dtype=jnp.int32)[None, :]
    ).astype(bf16)
    condition = jnp.dot(label_hot, class_table, preferred_element_type=f32) + time_embed(
        timesteps, model_width
    )
    cond_low = jax.nn.silu(condition).astype(bf16)
    cond_own = lax.dynamic_slice_in_dim(cond_low, first_image, IMG_DEV)
    mod_own = (
        jnp.einsum("wd,dcf->wcf", cond_own, ada_weight, preferred_element_type=f32)
        + ada_bias.astype(f32)[None]
    )
    mod_full = lax.all_gather(mod_own, "tp", axis=2, tiled=True)

    def row_full(stretch_id):
        return exact_dot(row_onehot, mod_full[:, stretch_id, :])

    def row_own(stretch_id):
        return exact_dot(row_onehot, mod_own[:, stretch_id, :])

    def input_grads(partial_rows, normed, inverse, scale):
        own_grad = column_sum(partial_rows)
        normed_own = own_cols(normed)
        scaled_grad = own_grad * (1.0 + own_cols(scale))
        mean_grad, mean_cross = lax.psum(
            (
                jnp.sum(scaled_grad, axis=1, keepdims=True) / model_width,
                jnp.sum(scaled_grad * normed_own, axis=1, keepdims=True) / model_width,
            ),
            "tp",
        )
        return (
            own_grad,
            own_grad * normed_own,
            inverse * (scaled_grad - mean_grad - normed_own * mean_cross),
        )

    picked = jnp.dot(
        place, jnp.concatenate([tokens, out_grad], axis=1), preferred_element_type=f32
    )
    rows_in = picked[:, :col_local].astype(bf16)
    grad_rows = picked[:, col_local:]
    gate_one = row_own(2)
    gate_two = row_own(5)
    mlp_grad = (grad_rows * gate_two).astype(bf16)
    full_in = whole_rows(rows_in).astype(f32)
    mlp_grad_full = whole_rows(mlp_grad)
    normed_one, inverse_one = norm_rows(full_in)
    scale_one = row_full(1)
    branch_one = (normed_one * (1.0 + scale_one) + row_full(0)).astype(bf16)
    qkv_bias = jnp.stack([qv_bias[0], jnp.zeros_like(qv_bias[0]), qv_bias[1]]).astype(f32)
    qkv_rows = (
        jnp.einsum("rd,dcf->rcf", branch_one, qkv_weight, preferred_element_type=f32)
        + qkv_bias[None]
    ).astype(bf16)
    query_all, key_all, value_all = (
        qkv_rows[:, part].reshape(ROWS, heads_local, HEAD_DIM) for part in range(3)
    )
    same_image = row_image[:, None] == row_image[None, :]
    raw = jnp.einsum("qhe,khe->hqk", query_all, key_all, preferred_element_type=f32) * scale_factor
    masked = jnp.where(same_image[None], raw, -1e30)
    top_score = jnp.max(masked, axis=2, keepdims=True)
    exp_scores = jnp.exp(masked - top_score)
    attn_probs = exp_scores / jnp.sum(exp_scores, axis=2, keepdims=True)
    probs_low = attn_probs.astype(bf16)
    attended = (
        jnp.einsum("hqk,khe->qhe", probs_low, value_all, preferred_element_type=f32)
        .reshape(ROWS, head_cols)
        .astype(bf16)
    )
    attn_out = column_sum(
        jnp.dot(attended, proj_weight, preferred_element_type=f32)
    ) + proj_bias.astype(f32)
    middle = rows_in.astype(f32) + gate_one * attn_out
    middle_full = whole_rows(middle.astype(bf16)).astype(f32)
    normed_two, inverse_two = norm_rows(middle_full)
    scale_two = row_full(4)
    branch_two = (normed_two * (1.0 + scale_two) + row_full(3)).astype(bf16)
    pre_act = jnp.dot(branch_two, hidden_weight, preferred_element_type=f32) + hidden_bias.astype(
        f32
    )
    act_low = gelu_tanh(pre_act).astype(bf16)
    mlp_out = column_sum(
        jnp.dot(act_low, output_weight, preferred_element_type=f32)
    ) + output_bias.astype(f32)
    final_rows = middle + gate_two * mlp_out
    output = reinsert(final_rows.astype(bf16), tokens)
    gate_two_rows = grad_rows * mlp_out
    output_bias_term = jnp.sum(mlp_grad, axis=0, dtype=f32)
    output_weight_term = jnp.einsum(
        "rf,rd->fd", act_low, mlp_grad_full, preferred_element_type=f32
    ).astype(bf16)
    act_grad = jnp.einsum("rd,fd->rf", mlp_grad_full, output_weight, preferred_element_type=f32)
    gelu_pull = jax.vjp(gelu_tanh, pre_act)[1]
    pre_grad = gelu_pull(act_grad)[0].astype(bf16)
    hidden_bias_term = jnp.sum(pre_grad, axis=0, dtype=f32)
    hidden_weight_term = jnp.einsum(
        "rd,rf->df", branch_two, pre_grad, preferred_element_type=f32
    ).astype(bf16)
    two_partial = jnp.einsum("rf,df->rd", pre_grad, hidden_weight, preferred_element_type=f32)
    shift_two_grad, scale_two_grad, two_norm_grad = input_grads(
        two_partial, normed_two, inverse_two, scale_two
    )
    middle_grad = grad_rows + two_norm_grad
    gate_one_rows = middle_grad * attn_out
    attn_grad = (middle_grad * gate_one).astype(bf16)
    proj_bias_term = jnp.sum(attn_grad, axis=0, dtype=f32)
    attn_grad_full = whole_rows(attn_grad)
    proj_weight_term = jnp.einsum(
        "rf,rd->fd", attended, attn_grad_full, preferred_element_type=f32
    ).astype(bf16)
    attended_grad = (
        jnp.einsum("rd,fd->rf", attn_grad_full, proj_weight, preferred_element_type=f32)
        .astype(bf16)
        .reshape(ROWS, heads_local, HEAD_DIM)
    )
    value_term = jnp.einsum("hqk,qhe->khe", probs_low, attended_grad, preferred_element_type=f32)
    prob_grad = jnp.einsum("qhe,khe->hqk", attended_grad, value_all, preferred_element_type=f32)
    row_dot = jnp.sum(attn_probs * prob_grad, axis=2, keepdims=True)
    score_grad = (attn_probs * (prob_grad - row_dot)).astype(bf16)
    query_term = (
        jnp.einsum("hqk,khe->qhe", score_grad, key_all, preferred_element_type=f32) * scale_factor
    )
    key_term = (
        jnp.einsum("hqk,qhe->khe", score_grad, query_all, preferred_element_type=f32)
        * scale_factor
    )
    qkv_grad = (
        jnp.stack([query_term, key_term, value_term], axis=1)
        .reshape(ROWS, 3, head_cols)
        .astype(bf16)
    )
    qkv_sums = jnp.sum(qkv_grad, axis=0, dtype=f32)
    qkv_weight_term = jnp.einsum(
        "rd,rcf->dcf", branch_one, qkv_grad, preferred_element_type=f32
    ).astype(bf16)
    one_partial = jnp.einsum("rcf,dcf->rd", qkv_grad, qkv_weight, preferred_element_type=f32)
    shift_one_grad, scale_one_grad, one_norm_grad = input_grads(
        one_partial, normed_one, inverse_one, scale_one
    )
    in_grad = middle_grad + one_norm_grad
    tokens_grad = reinsert(in_grad.astype(bf16), out_grad)
    per_row = jnp.concatenate(
        [
            shift_one_grad,
            scale_one_grad,
            gate_one_rows,
            shift_two_grad,
            scale_two_grad,
            gate_two_rows,
        ],
        axis=1,
    )
    mod_grad = jnp.einsum(
        "rw,rf->wf", row_onehot, per_row, precision=HIGHEST, preferred_element_type=f32
    )
    small = jnp.concatenate(
        [
            mod_grad.reshape(-1),
            qkv_sums[0],
            qkv_sums[2],
            proj_bias_term,
            hidden_bias_term,
            output_bias_term,
        ]
    )
    small_all = lax.all_gather(small, "seq", axis=0)
    mod_size = mod_grad.size
    mod_all = small_all[:, :mod_size].reshape(images, 6, col_local)
    bias_sums = jnp.sum(small_all[:, mod_size:], axis=0)
    ada_bias_grad = jnp.sum(mod_all, axis=0)
    qv_bias_grad = bias_sums[: 2 * col_local].reshape(2, col_local)
    at = 2 * col_local
    proj_bias_grad = bias_sums[at : at + col_local]
    at += col_local
    hidden_bias_grad = bias_sums[at : at + hidden_bias.shape[0]]
    at += hidden_bias.shape[0]
    output_bias_grad = bias_sums[at:]
    width_start = seq_index * slice_width
    cond_cols = lax.dynamic_slice_in_dim(condition, width_start, slice_width, 1)
    low_cols = lax.dynamic_slice_in_dim(cond_low, width_start, slice_width, 1)
    ada_weight_grad = jnp.einsum(
        "wd,wcf->dcf",
        low_cols.astype(f32),
        mod_all,
        precision=HIGHEST,
        preferred_element_type=f32,
    )
    ada_rows = lax.dynamic_slice_in_dim(ada_weight, width_start, slice_width, 0)
    cond_grad = lax.psum(
        jnp.einsum(
            "wcf,dcf->wd",
            mod_all,
            ada_rows.astype(f32),
            precision=HIGHEST,
            preferred_element_type=f32,
        ),
        "tp",
    )
    silu_pull = jax.vjp(jax.nn.silu, cond_cols)[1]
    class_grad = jnp.einsum(
        "wc,wd->cd",
        label_hot.astype(f32),
        silu_pull(cond_grad)[0],
        precision=HIGHEST,
        preferred_element_type=f32,
    )
    qkv_weight_grad, proj_weight_grad, hidden_weight_grad, output_weight_grad = (
        lax.psum_scatter(qkv_weight_term, "seq", scatter_dimension=0, tiled=True).astype(f32),
        lax.psum_scatter(proj_weight_term, "seq", scatter_dimension=1, tiled=True).astype(f32),
        lax.psum_scatter(hidden_weight_term, "seq", scatter_dimension=0, tiled=True).astype(f32),
        lax.psum_scatter(output_weight_term, "seq", scatter_dimension=1, tiled=True).astype(f32),
    )
    return (
        output,
        tokens_grad,
        class_grad,
        ada_weight_grad,
        ada_bias_grad,
        qkv_weight_grad,
        qv_bias_grad,
        proj_weight_grad,
        proj_bias_grad,
        hidden_weight_grad,
        hidden_bias_grad,
        output_weight_grad,
        output_bias_grad,
    )


def solution(mesh):
    return jax.shard_map(
        local,
        mesh=mesh,
        in_specs=(
            P("seq", "tp"),
            P("seq", "tp"),
            P("seq"),
            P(),
            P(),
            P(),
            P(),
            P(None, None, "tp"),
            P(None, "tp"),
            P(None, None, "tp"),
            P(None, "tp"),
            P("tp", None),
            P("tp"),
            P(None, "tp"),
            P("tp"),
            P("tp", None),
            P("tp"),
        ),
        out_specs=(
            P("seq", "tp"),
            P("seq", "tp"),
            P(None, "seq"),
            P("seq", None, "tp"),
            P(None, "tp"),
            P("seq", None, "tp"),
            P(None, "tp"),
            P("tp", "seq"),
            P("tp"),
            P("seq", "tp"),
            P("tp"),
            P("tp", "seq"),
            P("tp"),
        ),
        check_vma=False,
    )
```

```python
import functools
import math

import jax
import jax.numpy as jnp
from jax import lax
from jax.experimental import pallas as pl
from jax.experimental.pallas import tpu as pltpu
from jax.sharding import PartitionSpec as P

HEAD_DIM = 72
IMG_DEV = 4
ROWS = 640
PART = 160
TILE = 384
UNITS = 9
BLOCKS = 8
NORM_EPS = 1e-06
HIGHEST = lax.Precision.HIGHEST
MESH = pl.DeviceIdType.MESH
F32 = jnp.float32
BF16 = jnp.bfloat16


def mm(left, right):
    return jnp.dot(left, right, preferred_element_type=F32)


def mm_t(left, right):
    return lax.dot_general(left, right, (((1,), (1,)), ((), ())), preferred_element_type=F32)


def t_mm(left, right):
    return lax.dot_general(left, right, (((0,), (0,)), ((), ())), preferred_element_type=F32)


def norm_rows(values):
    centered = values - jnp.mean(values, axis=1, keepdims=True)
    inverse = lax.rsqrt(jnp.mean(centered * centered, axis=1, keepdims=True) + NORM_EPS)
    return centered * inverse, inverse


def norm_pull(normed, inverse, grad):
    return inverse * (
        grad
        - jnp.mean(grad, axis=1, keepdims=True)
        - normed * jnp.mean(grad * normed, axis=1, keepdims=True)
    )


def gelu_pair(values):
    coef = math.sqrt(2.0 / math.pi)
    square = values * values
    tanh = jnp.tanh(coef * (values + 0.044715 * (values * square)))
    half = 0.5 * (1.0 + tanh)
    slope = half + 0.5 * values * (1.0 - tanh * tanh) * (
        coef * (1.0 + (3.0 * 0.044715) * square)
    )
    return values * half, slope


def block_kernel(
    sizes,
    ends_ref,
    rank_row_ref,
    rank_col_ref,
    mod_ref,
    qkv_bias_ref,
    hidden_bias_ref,
    tokens_hbm,
    grad_hbm,
    wqkv_hbm,
    wproj_hbm,
    whid_hbm,
    wout_hbm,
    output_hbm,
    tokens_grad_hbm,
    small_ref,
    *rest,
):
    n_seq, width, cols, head_cols, ff, toks = sizes
    reduce_here = n_seq == BLOCKS
    if reduce_here:
        qkvg_ref, projg_ref, hidg_ref, outg_ref = rest[:4]
        rest = rest[4:]
    else:
        parts_hbm = rest[0]
        rest = rest[1:]
    (
        tok, dyt, wqkv, wproj, whid, wout,
        xg, dyg, modf, h1, h1t, qkvh, pbs, oh, oc, rsb, rv1, sd2, rv2,
        msb, mv1, md2, mv2, ag, h2t, dm, dmt, du, doh, dsb, dqkv,
        units, ry, rz, a_own, x1_own, n2_own, dx1_own, dy_own, smp, sms, smr, modr,
        in_sem, out_sem,
        ag_s, ag_r, rs_s, rs_r, mod_s, mod_r, fin_s, fin_r, sm_s, sm_r, sg_s, sg_r,
        y_s, y_r, z_s, z_r,
    ) = rest
    heads = head_cols // HEAD_DIM
    scale = HEAD_DIM ** (-0.5)
    g_act = h1

    seq = lax.axis_index("seq")
    t = lax.axis_index("tp")
    h, l = t // 2, t % 2
    hi, lo = seq // 2, seq % 2
    n_hi = n_seq // 2
    sib = t + 1 - 2 * l
    far = t + 2 - 4 * h
    diag = 3 - t

    def send(src, dst, ssem, rsem, where):
        copy = pltpu.make_async_remote_copy(
            src_ref=src, dst_ref=dst, send_sem=ssem, recv_sem=rsem,
            device_id=where, device_id_type=MESH,
        )
        copy.start()
        return copy

    def got(dst, ssem, rsem, where):
        pltpu.make_async_remote_copy(
            src_ref=dst, dst_ref=dst, send_sem=ssem, recv_sem=rsem,
            device_id=where, device_id_type=MESH,
        ).wait_recv()

    sent = []

    barrier = pltpu.get_barrier_semaphore()
    for k in range(1, 4):
        pl.semaphore_signal(
            barrier, inc=1, device_id={"tp": (t + k) % 4}, device_id_type=MESH
        )

    def greet(k, carry):
        pl.semaphore_signal(
            barrier, inc=1, device_id={"seq": (seq + k) % n_seq}, device_id_type=MESH
        )
        return carry

    lax.fori_loop(1, n_seq, greet, 0)

    loads = [
        pltpu.make_async_copy(src, dst, in_sem.at[i])
        for i, (src, dst) in enumerate(
            [
                (tokens_hbm, tok), (grad_hbm, dyt), (wqkv_hbm, wqkv),
                (wproj_hbm, wproj), (whid_hbm, whid), (wout_hbm, wout),
            ]
        )
    ]
    for load in loads:
        load.start()

    def rows_image(start, count):
        ids = lax.broadcasted_iota(jnp.int32, (count, 1), 0) + start
        image = jnp.zeros((count, 1), jnp.int32)
        for i in range(IMG_DEV):
            image += (ids >= ends_ref[i]).astype(jnp.int32)
        return image

    def mod_rows(which, image):
        out = jnp.zeros((image.shape[0], width), F32)
        for i in range(IMG_DEV):
            row = modf[pl.ds(which * IMG_DEV + i, 1), :]
            out = jnp.where(image == i, row, out)
        return out

    loads[0].wait()
    loads[1].wait()

    def pick(b, carry):
        ids = lax.broadcasted_iota(jnp.int32, (PART, toks), 0) + b * PART
        place = jnp.where(rank_row_ref[...] == ids, 1.0, 0.0).astype(BF16)
        at = pl.ds(pl.multiple_of(b * PART, PART), PART)
        xg[t, at, :] = mm(place, tok[...]).astype(BF16)
        dyg[t, at, :] = mm(place, dyt[...]).astype(BF16)
        return carry

    lax.fori_loop(0, 4, pick, 0)
    modr[t] = mod_ref[...]

    pl.semaphore_wait(barrier, 3 + n_seq - 1)

    def gather_start(buf, base):
        sent.append(send(buf.at[t], buf.at[t], ag_s.at[base], ag_r.at[base], {"tp": far}))
        sent.append(
            send(buf.at[t], buf.at[t], ag_s.at[base + 1], ag_r.at[base + 1], {"tp": sib})
        )

    def gather_pass(buf, base):
        got(buf.at[far], ag_s.at[base], ag_r.at[base], {"tp": far})
        sent.append(
            send(buf.at[far], buf.at[far], ag_s.at[base + 2], ag_r.at[base + 2], {"tp": sib})
        )

    def gather_end(buf, base):
        got(buf.at[sib], ag_s.at[base + 1], ag_r.at[base + 1], {"tp": sib})
        got(buf.at[diag], ag_s.at[base + 2], ag_r.at[base + 2], {"tp": sib})

    gather_start(xg, 0)
    for k in range(1, 4):
        to = (t + k) % 4
        sent.append(
            send(modr.at[t], modr.at[t], mod_s.at[k - 1], mod_r.at[k - 1], {"tp": to})
        )
    gather_start(dyg, 3)
    for k in range(1, 4):
        source = (t + 4 - k) % 4
        got(modr.at[source], mod_s.at[k - 1], mod_r.at[k - 1], {"tp": source})
    for d in range(4):
        modf[:, d * cols : (d + 1) * cols] = modr[d]
    gather_pass(xg, 0)
    gather_end(xg, 0)

    def full_rows(slots, at):
        return jnp.concatenate([slots[d, at, :].astype(F32) for d in range(4)], axis=1)

    def norm_one(b, carry):
        at = pl.ds(pl.multiple_of(b * PART, PART), PART)
        image = rows_image(b * PART, PART)
        normed, _ = norm_rows(full_rows(xg, at))
        h1[at, :] = (normed * (1.0 + mod_rows(1, image)) + mod_rows(0, image)).astype(BF16)
        return carry

    lax.fori_loop(0, 4, norm_one, 0)
    gather_pass(dyg, 3)

    loads[2].wait()

    def project(b, carry):
        at = pl.ds(pl.multiple_of(b * 320, 320), 320)
        rows = (mm(h1[at, :], wqkv[...]) + qkv_bias_ref[...]).astype(BF16)
        for i in range(3 * heads):
            qkvh[i, at, :] = rows[:, i * HEAD_DIM : (i + 1) * HEAD_DIM]
        return carry

    lax.fori_loop(0, 2, project, 0)

    image_row = jnp.zeros((1, ROWS), jnp.int32)
    row_ids = lax.broadcasted_iota(jnp.int32, (1, ROWS), 1)
    for i in range(IMG_DEV):
        image_row += (row_ids >= ends_ref[i]).astype(jnp.int32)

    def attend(step, carry):
        hd, b = step // 4, step % 4
        at = pl.ds(pl.multiple_of(b * PART, PART), PART)
        scores = mm_t(qkvh[hd, at, :], qkvh[heads + hd]) * scale
        masked = jnp.where(rows_image(b * PART, PART) == image_row, scores, -1e30)
        exps = jnp.exp(masked - jnp.max(masked, axis=1, keepdims=True))
        probs = (exps / jnp.sum(exps, axis=1, keepdims=True)).astype(BF16)
        pbs[hd, at, :] = probs
        oh[hd, at, :] = mm(probs, qkvh[2 * heads + hd]).astype(BF16)
        return carry

    lax.fori_loop(0, 4 * heads, attend, 0)
    for hd in range(heads):
        oc[:, hd * HEAD_DIM : (hd + 1) * HEAD_DIM] = oh[hd]

    def store_blocks(buf, tile_at, values):
        low = values.astype(BF16)
        for b in range(4):
            buf[b % 2, b // 2, :, tile_at] = low[b * PART : (b + 1) * PART]

    def scatter_start(buf, first, base):
        sent.append(
            send(buf.at[1 - l, 1 - h], first.at[1 - h], rs_s.at[base], rs_r.at[base], {"tp": sib})
        )
        sent.append(
            send(buf.at[1 - l, h], first.at[h], rs_s.at[base + 1], rs_r.at[base + 1], {"tp": sib})
        )

    def scatter_pass(buf, first, mid, second, base):
        got(first.at[1 - h], rs_s.at[base], rs_r.at[base], {"tp": sib})
        mid[...] = (buf[l, 1 - h].astype(F32) + first[1 - h].astype(F32)).astype(BF16)
        sent.append(send(mid, second, rs_s.at[base + 2], rs_r.at[base + 2], {"tp": far}))

    def scatter_end(buf, first, second, base):
        got(first.at[h], rs_s.at[base + 1], rs_r.at[base + 1], {"tp": sib})
        got(second, rs_s.at[base + 2], rs_r.at[base + 2], {"tp": far})
        return (
            buf[l, h].astype(F32) + first[h].astype(F32) + second[...].astype(F32)
        )

    def finish_sends():
        for copy in sent:
            copy.wait_send()
        sent.clear()

    def tile(j):
        return pl.ds(pl.multiple_of(j * TILE, TILE), TILE)

    loads[3].wait()

    def branch_one(j, carry):
        store_blocks(rsb, tile(j), mm(oc[...], wproj[:, tile(j)]))
        return carry

    lax.fori_loop(0, width // TILE, branch_one, 0)
    scatter_start(rsb, rv1, 0)
    gather_end(dyg, 3)
    scatter_pass(rsb, rv1, sd2, rv2, 0)

    def out_cotangent(b, carry):
        at = pl.ds(pl.multiple_of(b * PART, PART), PART)
        image = rows_image(b * PART, PART)
        dm[at, :] = (full_rows(dyg, at) * mod_rows(5, image)).astype(BF16)
        return carry

    lax.fori_loop(0, 4, out_cotangent, 0)
    own = pl.ds(pl.multiple_of(t * PART, PART), PART)
    own_image = rows_image(t * PART, PART)
    dy_own[...] = full_rows(dyg, own)

    attn_out = scatter_end(rsb, rv1, rv2, 0) + modf[24:25, :]
    a_own[...] = attn_out
    middle = full_rows(xg, own) + mod_rows(2, own_image) * attn_out
    x1_own[...] = middle
    normed_two, inverse_two = norm_rows(middle.astype(BF16).astype(F32))
    n2_own[...] = normed_two
    ag[t] = (normed_two * (1.0 + mod_rows(4, own_image)) + mod_rows(3, own_image)).astype(BF16)
    gather_start(ag, 6)
    h1t[...] = h1[...].T
    gather_pass(ag, 6)
    dmt[...] = dm[...].T
    gather_end(ag, 6)
    loads[4].wait()
    loads[5].wait()

    def whole(buf):
        return jnp.concatenate([buf[b] for b in range(4)], axis=0)

    hb_rows = []

    def mlp(j, carry):
        at = tile(j)
        act, slope = gelu_pair(mm(whole(ag), whid[:, at]) + hidden_bias_ref[:, at])
        g_act[:, at] = act.astype(BF16)
        back = (slope * mm_t(dm[...], wout[at, :])).astype(BF16)
        du[:, at] = back
        return carry

    lax.fori_loop(0, ff // TILE, mlp, 0)
    h2t[...] = whole(ag).T
    finish_sends()

    def two_back(j, carry):
        store_blocks(rsb, tile(j), mm_t(du[...], whid[tile(j), :]))
        return carry

    lax.fori_loop(0, width // TILE, two_back, 0)
    scatter_start(rsb, rv1, 3)

    def branch_two(j, carry):
        store_blocks(msb, tile(j), mm(g_act[...], wout[:, tile(j)]))
        return carry

    lax.fori_loop(0, width // TILE, branch_two, 0)
    scatter_pass(rsb, rv1, sd2, rv2, 3)
    scatter_start(msb, mv1, 6)

    y_copies = {}

    def put_unit(unit, values, at):
        low = values.astype(BF16)
        step = width // BLOCKS
        for j in range(BLOCKS):
            units[unit, j % 2, j // 2, :, at] = low[j * step : (j + 1) * step]

    def unit_send(unit):
        if reduce_here:
            y_copies[unit] = send(
                units.at[unit, 1 - lo], ry.at[unit], y_s.at[unit], y_r.at[unit],
                {"seq": seq + 1 - 2 * lo},
            )
        else:
            copy = pltpu.make_async_copy(units.at[unit], parts_hbm.at[unit], y_s.at[unit])
            copy.start()
            y_copies[unit] = copy

    z_copies = []

    def unit_pass(unit):
        if not reduce_here:
            return
        got(ry.at[unit], y_s.at[unit], y_r.at[unit], {"seq": seq + 1 - 2 * lo})
        for k in range(n_hi):
            units[unit, lo, k] = (
                units[unit, lo, k].astype(F32) + ry[unit, k].astype(F32)
            ).astype(BF16)
        for k in range(1, n_hi):
            peer = (hi + k) % n_hi
            z_copies.append(
                send(
                    units.at[unit, lo, peer], rz.at[unit, k - 1],
                    z_s.at[unit, k - 1], z_r.at[unit, k - 1], {"seq": 2 * peer + lo},
                )
            )

    def unit_end(unit):
        total = units[unit, lo, hi].astype(F32)
        for k in range(1, n_hi):
            source = (hi + n_hi - k) % n_hi
            got(
                rz.at[unit, k - 1], z_s.at[unit, k - 1], z_r.at[unit, k - 1],
                {"seq": 2 * source + lo},
            )
            total += rz[unit, k - 1].astype(F32)
        return total

    for j in range(3):
        put_unit(j, mm(dmt[...], g_act[:, j * TILE : (j + 1) * TILE]), slice(None))
        unit_send(j)

    def segments(which, values):
        for i in range(IMG_DEV):
            smp[which * IMG_DEV + i : which * IMG_DEV + i + 1, :] = jnp.sum(
                jnp.where(own_image == i, values, 0.0), axis=0, keepdims=True
            )

    smp[24:32, :] = jnp.zeros((8, width), F32)
    own_grad = scatter_end(rsb, rv1, rv2, 3)
    segments(3, own_grad)
    segments(4, own_grad * n2_own[...])
    middle_grad = dy_own[...] + norm_pull(
        n2_own[...], inverse_two, own_grad * (1.0 + mod_rows(4, own_image))
    )
    dx1_own[...] = middle_grad
    segments(2, middle_grad * a_own[...])
    attn_grad = (middle_grad * mod_rows(2, own_image)).astype(BF16)
    ag[t] = attn_grad
    gather_start(ag, 9)
    smp[24:25, :] = jnp.sum(attn_grad.astype(F32), axis=0, keepdims=True)
    smp[25:26, :] = jnp.sum(
        (dy_own[...] * mod_rows(5, own_image)).astype(BF16).astype(F32), axis=0, keepdims=True
    )
    put_unit(3, mm(h2t[...], du[:, 0:TILE]), slice(None))
    unit_send(3)
    gather_pass(ag, 9)
    for j in range(1, 3):
        put_unit(3 + j, mm(h2t[...], du[:, j * TILE : (j + 1) * TILE]), slice(None))
        unit_send(3 + j)
    scatter_pass(msb, mv1, md2, mv2, 6)
    gather_end(ag, 9)

    def back_heads(b, carry):
        at = pl.ds(pl.multiple_of(b * PART, PART), PART)
        rows = mm_t(ag[b], wproj[...]).astype(BF16)
        for hd in range(heads):
            doh[hd, at, :] = rows[:, hd * HEAD_DIM : (hd + 1) * HEAD_DIM]
        return carry

    lax.fori_loop(0, 4, back_heads, 0)
    unit_pass(0)
    unit_pass(1)

    def attend_back(hd, carry):
        def one(b, inner):
            at = pl.ds(pl.multiple_of(b * PART, PART), PART)
            probs = pbs[hd, at, :].astype(F32)
            prob_grad = mm_t(doh[hd, at, :], qkvh[2 * heads + hd])
            row_dot = jnp.sum(probs * prob_grad, axis=1, keepdims=True)
            score_grad = (probs * (prob_grad - row_dot)).astype(BF16)
            dsb[at, :] = score_grad
            oh[hd, at, :] = (mm(score_grad, qkvh[heads + hd]) * scale).astype(BF16)
            return inner

        lax.fori_loop(0, 4, one, 0)
        qkvh[heads + hd] = (t_mm(qkvh[hd], dsb[...]) * scale).T.astype(BF16)
        qkvh[2 * heads + hd] = t_mm(doh[hd], pbs[hd]).T.astype(BF16)
        return carry

    lax.fori_loop(0, heads, attend_back, 0)
    for i in range(3 * heads):
        dqkv[:, i * HEAD_DIM : (i + 1) * HEAD_DIM] = oh[i] if i < heads else qkvh[i]
    finish_sends()

    def one_back(j, carry):
        store_blocks(rsb, tile(j), mm_t(dqkv[...], wqkv[tile(j), :]))
        return carry

    lax.fori_loop(0, width // TILE, one_back, 0)
    scatter_start(rsb, rv1, 9)

    mlp_out = scatter_end(msb, mv1, mv2, 6) + modf[25:26, :]
    segments(5, dy_own[...] * mlp_out)
    final = (x1_own[...] + mod_rows(5, own_image) * mlp_out).astype(BF16)

    def columns_start(rows, base, src_at, dst_at):
        for d in range(4):
            dyg[d, src_at, :] = rows[:, d * cols : (d + 1) * cols]
        dyg[t, dst_at, :] = dyg[t, src_at, :]
        for k in range(1, 4):
            to = (t + k) % 4
            sent.append(
                send(
                    dyg.at[to, src_at], dyg.at[t, dst_at],
                    fin_s.at[base + k - 1], fin_r.at[base + k - 1], {"tp": to},
                )
            )

    def columns_end(base, dst_at):
        for k in range(1, 4):
            source = (t + 4 - k) % 4
            got(
                dyg.at[source, dst_at], fin_s.at[base + k - 1], fin_r.at[base + k - 1],
                {"tp": source},
            )
        return jnp.concatenate([dyg[d, dst_at, :] for d in range(4)], axis=0)

    def place_back(rows, initial):
        def one(b, carry):
            at = pl.ds(pl.multiple_of(b * 256, 256), 256)
            rank = rank_col_ref[at, :]
            ids = lax.broadcasted_iota(jnp.int32, (256, ROWS), 1)
            place = jnp.where(rank == ids, 1.0, 0.0).astype(BF16)
            placed = mm(place, rows)
            initial[at, :] = jnp.where(rank >= 0, placed, initial[at, :].astype(F32)).astype(
                BF16
            )
            return carry

        lax.fori_loop(0, toks // 256, one, 0)

    parts_at = [pl.ds(i * PART, PART) for i in range(4)]
    scatter_pass(rsb, rv1, sd2, rv2, 9)
    columns_start(final, 0, parts_at[2], parts_at[0])

    unit_pass(2)
    h2t[...] = whole(ag).T
    for j in range(2):
        put_unit(6 + j, mm(h1t[...], dqkv[:, j * TILE : (j + 1) * TILE]), slice(None))
        unit_send(6 + j)
    tail = 3 * head_cols - 2 * TILE
    put_unit(8, mm(h1t[...], dqkv[:, 2 * TILE :]), slice(0, tail))
    put_unit(8, mm(h2t[...], oc[...]), slice(tail, TILE))
    unit_send(8)
    unit_pass(3)

    own_grad = scatter_end(rsb, rv1, rv2, 9)
    normed_one, inverse_one = norm_rows(full_rows(xg, own))
    in_grad = dx1_own[...] + norm_pull(
        normed_one, inverse_one, own_grad * (1.0 + mod_rows(1, own_image))
    )
    columns_start(in_grad.astype(BF16), 3, parts_at[3], parts_at[1])
    segments(0, own_grad)
    segments(1, own_grad * normed_one)

    for d in range(4):
        sms[d] = smp[:, d * cols : (d + 1) * cols]
    for k in range(1, 4):
        to = (t + k) % 4
        sent.append(
            send(sms.at[to], smr.at[t], sm_s.at[k - 1], sm_r.at[k - 1], {"tp": to})
        )
    place_back(columns_end(0, parts_at[0]), tok)
    out_copy = pltpu.make_async_copy(tok, output_hbm, out_sem.at[0])
    out_copy.start()
    unit_pass(4)
    total = sms[t]
    for k in range(1, 4):
        source = (t + 4 - k) % 4
        got(smr.at[source], sm_s.at[k - 1], sm_r.at[k - 1], {"tp": source})
        total += smr[source]
    qkv_sum = jnp.sum(dqkv[...].astype(F32), axis=0, keepdims=True)
    hid_sum = jnp.sum(du[...].astype(F32), axis=0, keepdims=True)
    small_ref[seq] = total
    small_ref[seq, 26:27, :] = qkv_sum[:, 0:head_cols]
    small_ref[seq, 27:28, :] = qkv_sum[:, 2 * head_cols : 3 * head_cols]
    for d in range(4):
        small_ref[seq, 28 + d : 29 + d, :] = hid_sum[:, d * cols : (d + 1) * cols]

    def tell(k, carry):
        pltpu.make_async_remote_copy(
            src_ref=small_ref.at[seq], dst_ref=small_ref.at[seq],
            send_sem=sg_s.at[k], recv_sem=sg_r.at[k],
            device_id={"seq": (seq + k) % n_seq}, device_id_type=MESH,
        ).start()
        return carry

    lax.fori_loop(1, n_seq, tell, 0)
    unit_pass(5)
    place_back(columns_end(3, parts_at[1]), dyt)
    grad_copy = pltpu.make_async_copy(dyt, tokens_grad_hbm, out_sem.at[1])
    grad_copy.start()
    for unit in range(6, UNITS):
        unit_pass(unit)
    if reduce_here:
        for j in range(3):
            outg_ref[j * TILE : (j + 1) * TILE, :] = unit_end(j).T
            hidg_ref[:, j * TILE : (j + 1) * TILE] = unit_end(3 + j)
        for j in range(2):
            qkvg_ref[:, j * TILE : (j + 1) * TILE] = unit_end(6 + j)
        last = unit_end(8)
        qkvg_ref[:, 2 * TILE : 2 * TILE + tail] = last[:, :tail]
        projg_ref[...] = last[:, tail:].T

    def hear(k, carry):
        source = (seq + n_seq - k) % n_seq
        copy = pltpu.make_async_remote_copy(
            src_ref=small_ref.at[seq], dst_ref=small_ref.at[source],
            send_sem=sg_s.at[k], recv_sem=sg_r.at[k],
            device_id={"seq": (seq + k) % n_seq}, device_id_type=MESH,
        )
        copy.wait_recv()
        copy.wait_send()
        return carry

    lax.fori_loop(1, n_seq, hear, 0)
    finish_sends()
    for copy in z_copies:
        copy.wait_send()
    for copy in y_copies.values():
        if reduce_here:
            copy.wait_send()
        else:
            copy.wait()
    out_copy.wait()
    grad_copy.wait()


def run_block(sizes, *operands):
    n_seq, width, cols, head_cols, ff, toks = sizes
    heads = head_cols // HEAD_DIM
    reduce_here = n_seq == BLOCKS
    step = width // BLOCKS
    vmem, dma = pltpu.VMEM, pltpu.SemaphoreType.DMA
    any_spec = pl.BlockSpec(memory_space=pl.ANY)
    vmem_spec = pl.BlockSpec(memory_space=pltpu.VMEM)
    out_shape = [
        jax.ShapeDtypeStruct((toks, cols), BF16),
        jax.ShapeDtypeStruct((toks, cols), BF16),
        jax.ShapeDtypeStruct((n_seq, 32, cols), F32),
    ]
    out_specs = [any_spec, any_spec, vmem_spec]
    if reduce_here:
        out_shape += [
            jax.ShapeDtypeStruct((step, 3 * head_cols), F32),
            jax.ShapeDtypeStruct((head_cols, step), F32),
            jax.ShapeDtypeStruct((step, ff), F32),
            jax.ShapeDtypeStruct((ff, step), F32),
        ]
        out_specs += [vmem_spec] * 4
    else:
        out_shape.append(jax.ShapeDtypeStruct((UNITS, 2, BLOCKS // 2, step, TILE), BF16))
        out_specs.append(any_spec)
    own = vmem((PART, width), F32)
    low = vmem((ROWS, width), BF16)
    high = vmem((width, ROWS), BF16)
    scratch = [
        vmem((toks, cols), BF16), vmem((toks, cols), BF16),
        vmem((width, 3 * head_cols), BF16), vmem((head_cols, width), BF16),
        vmem((width, ff), BF16), vmem((ff, width), BF16),
        vmem((4, ROWS, cols), BF16), vmem((4, ROWS, cols), BF16),
        vmem((32, width), F32), low, high,
        vmem((3 * heads, ROWS, HEAD_DIM), BF16), vmem((heads, ROWS, ROWS), BF16),
        vmem((heads, ROWS, HEAD_DIM), BF16), vmem((ROWS, head_cols), BF16),
        vmem((2, 2, PART, width), BF16), vmem((2, PART, width), BF16),
        vmem((PART, width), BF16), vmem((PART, width), BF16),
        vmem((2, 2, PART, width), BF16), vmem((2, PART, width), BF16),
        vmem((PART, width), BF16), vmem((PART, width), BF16),
        vmem((4, PART, width), BF16), high, low, high, vmem((ROWS, ff), BF16),
        vmem((heads, ROWS, HEAD_DIM), BF16), vmem((ROWS, ROWS), BF16),
        vmem((ROWS, 3 * head_cols), BF16),
        vmem((UNITS, 2, BLOCKS // 2, step, TILE), BF16),
        vmem((UNITS if reduce_here else 1, BLOCKS // 2, step, TILE), BF16),
        vmem((UNITS if reduce_here else 1, BLOCKS // 2 - 1, step, TILE), BF16),
        own, own, own, own, own,
        vmem((32, width), F32), vmem((4, 32, cols), F32), vmem((4, 32, cols), F32),
        vmem((4, 32, cols), F32),
        dma((6,)), dma((2,)),
        dma((12,)), dma((12,)), dma((12,)), dma((12,)), dma((3,)), dma((3,)),
        dma((6,)), dma((6,)), dma((3,)), dma((3,)), dma((n_seq,)), dma((n_seq,)),
        dma((UNITS,)), dma((UNITS,)), dma((UNITS, BLOCKS // 2 - 1)), dma((UNITS, BLOCKS // 2 - 1)),
    ]
    return pl.pallas_call(
        functools.partial(block_kernel, sizes),
        out_shape=out_shape,
        in_specs=[pl.BlockSpec(memory_space=pltpu.SMEM)] + [vmem_spec] * 5 + [any_spec] * 6,
        out_specs=out_specs,
        scratch_shapes=scratch,
        compiler_params=pltpu.CompilerParams(
            collective_id=0, has_side_effects=True, vmem_limit_bytes=63 * 1024 * 1024
        ),
    )(*operands)


def exact_dot(left_mat, right_mat):
    return jnp.dot(left_mat, right_mat, precision=HIGHEST, preferred_element_type=F32)


def time_embed(step_ids, model_width):
    half_width = model_width // 2
    frequency = jnp.exp(-math.log(10000.0) * jnp.arange(half_width, dtype=F32) / half_width)
    angles = step_ids.astype(F32)[:, None] * frequency[None, :]
    return jnp.concatenate([jnp.cos(angles), jnp.sin(angles)], axis=1)


def local(
    tokens,
    out_grad,
    route_mask,
    kept_counts,
    labels,
    timesteps,
    class_table,
    ada_weight,
    ada_bias,
    qkv_weight,
    qv_bias,
    proj_weight,
    proj_bias,
    hidden_weight,
    hidden_bias,
    output_weight,
    output_bias,
):
    seq_index = lax.axis_index("seq")
    n_seq = lax.axis_size("seq")
    toks, cols = tokens.shape
    width = class_table.shape[1]
    head_cols = qkv_weight.shape[2]
    ff = hidden_weight.shape[1]
    images = kept_counts.shape[0]
    slice_width = width // n_seq
    first_image = seq_index * IMG_DEV
    own_ends = jnp.cumsum(lax.dynamic_slice_in_dim(kept_counts, first_image, IMG_DEV))
    rank = jnp.where(route_mask > 0, jnp.cumsum(route_mask) - 1, -1)

    label_hot = (
        labels[:, None] == jnp.arange(class_table.shape[0], dtype=jnp.int32)[None, :]
    ).astype(BF16)
    condition = mm(label_hot, class_table) + time_embed(timesteps, width)
    cond_low = jax.nn.silu(condition).astype(BF16)
    cond_own = lax.dynamic_slice_in_dim(cond_low, first_image, IMG_DEV)
    mod_own = (
        jnp.einsum("wd,dcf->cwf", cond_own, ada_weight, preferred_element_type=F32)
        + ada_bias.astype(F32)[:, None]
    )
    mod_rows = jnp.concatenate(
        [
            mod_own.reshape(6 * IMG_DEV, cols),
            proj_bias.astype(F32)[None],
            output_bias.astype(F32)[None],
            jnp.zeros((6, cols), F32),
        ]
    )
    qkv_bias = jnp.concatenate([qv_bias[0], jnp.zeros_like(qv_bias[0]), qv_bias[1]])

    results = run_block(
        (n_seq, width, cols, head_cols, ff, toks),
        own_ends.astype(jnp.int32),
        rank[None, :],
        rank[:, None],
        mod_rows,
        qkv_bias.astype(F32)[None],
        hidden_bias.astype(F32)[None],
        tokens,
        out_grad,
        qkv_weight.reshape(width, 3 * head_cols),
        proj_weight,
        hidden_weight,
        output_weight,
    )
    output, tokens_grad, small = results[:3]
    if n_seq == BLOCKS:
        qkv_weight_grad, proj_weight_grad, hidden_weight_grad, output_weight_grad = results[3:]
    else:
        parts = results[3].transpose(2, 1, 3, 0, 4).reshape(width, UNITS * TILE)
        summed = lax.psum_scatter(parts, "seq", scatter_dimension=0, tiled=True).astype(F32)
        output_weight_grad = summed[:, :ff].T
        hidden_weight_grad = summed[:, ff : 2 * ff]
        qkv_weight_grad = summed[:, 2 * ff : 2 * ff + 3 * head_cols]
        proj_weight_grad = summed[:, 2 * ff + 3 * head_cols :].T
    qkv_weight_grad = qkv_weight_grad.reshape(slice_width, 3, head_cols)

    mod_all = (
        small[:, : 6 * IMG_DEV]
        .reshape(n_seq, 6, IMG_DEV, cols)
        .transpose(0, 2, 1, 3)
        .reshape(images, 6, cols)
    )
    sums = jnp.sum(small[:, 24:], axis=0)
    ada_bias_grad = jnp.sum(mod_all, axis=0)
    proj_bias_grad = sums[0]
    output_bias_grad = sums[1]
    qv_bias_grad = sums[2:4]
    hidden_bias_grad = sums[4:].reshape(ff)
    width_start = seq_index * slice_width
    cond_cols = lax.dynamic_slice_in_dim(condition, width_start, slice_width, 1)
    low_cols = lax.dynamic_slice_in_dim(cond_low, width_start, slice_width, 1)
    ada_weight_grad = jnp.einsum(
        "wd,wcf->dcf",
        low_cols.astype(F32),
        mod_all,
        precision=HIGHEST,
        preferred_element_type=F32,
    )
    ada_rows = lax.dynamic_slice_in_dim(ada_weight, width_start, slice_width, 0)
    cond_grad = lax.psum(
        jnp.einsum(
            "wcf,dcf->wd",
            mod_all,
            ada_rows.astype(F32),
            precision=HIGHEST,
            preferred_element_type=F32,
        ),
        "tp",
    )
    silu_pull = jax.vjp(jax.nn.silu, cond_cols)[1]
    class_grad = exact_dot(label_hot.astype(F32).T, silu_pull(cond_grad)[0])
    return (
        output,
        tokens_grad,
        class_grad,
        ada_weight_grad,
        ada_bias_grad,
        qkv_weight_grad,
        qv_bias_grad,
        proj_weight_grad,
        proj_bias_grad,
        hidden_weight_grad,
        hidden_bias_grad,
        output_weight_grad,
        output_bias_grad,
    )


def solution(mesh):
    return jax.shard_map(
        local,
        mesh=mesh,
        in_specs=(
            P("seq", "tp"),
            P("seq", "tp"),
            P("seq"),
            P(),
            P(),
            P(),
            P(),
            P(None, None, "tp"),
            P(None, "tp"),
            P(None, None, "tp"),
            P(None, "tp"),
            P("tp", None),
            P("tp"),
            P(None, "tp"),
            P("tp"),
            P("tp", None),
            P("tp"),
        ),
        out_specs=(
            P("seq", "tp"),
            P("seq", "tp"),
            P(None, "seq"),
            P("seq", None, "tp"),
            P(None, "tp"),
            P("seq", None, "tp"),
            P(None, "tp"),
            P("tp", "seq"),
            P("tp"),
            P("seq", "tp"),
            P("tp"),
            P("tp", "seq"),
            P("tp"),
        ),
        check_vma=False,
    )
```

```python
import functools
import math

import jax
import jax.numpy as jnp
from jax import lax
from jax.experimental import pallas as pl
from jax.experimental.pallas import tpu as pltpu
from jax.sharding import PartitionSpec as P

HEAD_DIM = 72
IMG_DEV = 4
KEEP_MOST = 192
ROWS = 640
PART = 160
TILE = 384
UNITS = 9
SLOTS = 6
Z_FIRST = (3, 7)
BLOCKS = 8
NORM_EPS = 1e-06
HIGHEST = lax.Precision.HIGHEST
MESH = pl.DeviceIdType.MESH
F32 = jnp.float32
BF16 = jnp.bfloat16


def mm(left, right):
    return jnp.dot(left, right, preferred_element_type=F32)


def mm_t(left, right):
    return lax.dot_general(left, right, (((1,), (1,)), ((), ())), preferred_element_type=F32)


def t_mm(left, right):
    return lax.dot_general(left, right, (((0,), (0,)), ((), ())), preferred_element_type=F32)


def parts_of(values, count):
    parts = []
    for _ in range(count):
        part = values.astype(BF16)
        parts.append(part)
        values = values - part.astype(F32)
    return parts


def norm_rows(values):
    centered = values - jnp.mean(values, axis=1, keepdims=True)
    inverse = lax.rsqrt(jnp.mean(centered * centered, axis=1, keepdims=True) + NORM_EPS)
    return centered * inverse, inverse


def norm_pull(normed, inverse, grad):
    return inverse * (
        grad
        - jnp.mean(grad, axis=1, keepdims=True)
        - normed * jnp.mean(grad * normed, axis=1, keepdims=True)
    )


def gelu_pair(values):
    coef = math.sqrt(2.0 / math.pi)
    square = values * values
    tanh = jnp.tanh(coef * (values + 0.044715 * (values * square)))
    half = 0.5 * (1.0 + tanh)
    slope = half + 0.5 * values * (1.0 - tanh * tanh) * (
        coef * (1.0 + (3.0 * 0.044715) * square)
    )
    return values * half, slope


def block_kernel(
    sizes,
    counts_ref,
    mask_ref,
    cond_ref,
    labels_ref,
    bias_ref,
    tokens_hbm,
    grad_hbm,
    ada_hbm,
    wqkv_hbm,
    wproj_hbm,
    whid_hbm,
    wout_hbm,
    output_hbm,
    tokens_grad_hbm,
    classg_ref,
    adag_ref,
    adabg_ref,
    qvg_ref,
    projbg_ref,
    outbg_ref,
    hidbg_ref,
    *rest,
):
    n_seq, width, cols, head_cols, ff, toks, images, classes = sizes
    reduce_here = n_seq == BLOCKS
    slice_width = width // n_seq
    if reduce_here:
        qkvg_ref, projg_ref, hidg_ref, outg_ref = rest[:4]
        rest = rest[4:]
    else:
        parts_hbm = rest[0]
        rest = rest[1:]
    (
        tok, dyt, wqkv, wproj, whid, wout, rank_row,
        xg, dyg, modf, h1, h1t, qkvh, pbs, oh, oc, rsb, rv1, sd2, rv2,
        msb, mv1, md2, mv2, ag, h2t, dm, dmt, du, doh, dqkv,
        units, ry, rz, fin_in, fin_out, x_own, a_own, x1_own, n2_own, dx1_own, dy_own,
        smp, sms, smr, modr, sgr, cgr, slice_sel, slope_cols, act_cols, label_hot,
        in_sem, ada_sem, out_sem,
        ag_s, ag_r, rs_s, rs_r, mod_s, mod_r, fin_s, fin_r, sm_s, sm_r, cg_s, cg_r, sg_s, sg_r,
        y_s, y_r, z_s, z_r,
    ) = rest
    heads = head_cols // HEAD_DIM
    scale = HEAD_DIM ** (-0.5)
    g_act = h1
    x_nat = h1
    dy_nat = dm
    dsb = dmt

    seq = lax.axis_index("seq")
    t = lax.axis_index("tp")
    h, l = t // 2, t % 2
    bits = (seq % 2, (seq // 2) % 2, (seq // 4) % 2)
    sib = t + 1 - 2 * l
    far = t + 2 - 4 * h
    diag = 3 - t

    sems = {
        "ag": (ag_s, ag_r), "rs": (rs_s, rs_r), "mod": (mod_s, mod_r), "fin": (fin_s, fin_r),
        "sm": (sm_s, sm_r), "y": (y_s, y_r), "z": (z_s, z_r), "cg": (cg_s, cg_r),
    }

    def remote(src, dst, kind, index, where):
        ssem, rsem = sems[kind]
        return pltpu.make_async_remote_copy(
            src_ref=src, dst_ref=dst, send_sem=ssem.at[index], recv_sem=rsem.at[index],
            device_id=where, device_id_type=MESH,
        )

    def send(src, dst, kind, index, where):
        copy = remote(src, dst, kind, index, where)
        copy.start()
        return copy

    def got(dst, kind, index, where):
        remote(dst, dst, kind, index, where).wait_recv()

    sent = []
    y_copies = {}
    z_copies = {}

    def finish_sends():
        for copy in sent:
            copy.wait_send()
        sent.clear()

    barrier = pltpu.get_barrier_semaphore()
    for k in range(1, 4):
        pl.semaphore_signal(
            barrier, inc=1, device_id={"tp": (t + k) % 4}, device_id_type=MESH
        )

    def greet(k, carry):
        pl.semaphore_signal(
            barrier, inc=1, device_id={"seq": (seq + k) % n_seq}, device_id_type=MESH
        )
        return carry

    lax.fori_loop(1, n_seq, greet, 0)

    ada_spots = [
        buf.at[pl.ds(part * cols, cols)] for buf in (dm, du, h1) for part in range(2)
    ]

    def ada_loads():
        copies = [
            pltpu.make_async_copy(
                ada_hbm.at[pl.ds(j * cols, cols)], ada_spots[j], ada_sem.at[j]
            )
            for j in range(6)
        ]
        for copy in copies:
            copy.start()
        return copies

    loads = [
        pltpu.make_async_copy(src, dst, in_sem.at[i])
        for i, (src, dst) in enumerate(
            [
                (tokens_hbm, tok), (grad_hbm, dyt), (wqkv_hbm, wqkv),
                (wproj_hbm, wproj), (whid_hbm, whid), (wout_hbm, wout),
            ]
        )
    ]
    loads[0].start()
    loads[1].start()
    ada_copies = ada_loads()
    for load in loads[2:]:
        load.start()

    ends = []
    for i in range(IMG_DEV):
        count = counts_ref[seq * IMG_DEV + i]
        ends.append(count if i == 0 else ends[-1] + count)

    def rows_image(start, count):
        ids = lax.broadcasted_iota(jnp.int32, (count, 1), 0) + start
        image = jnp.zeros((count, 1), jnp.int32)
        for i in range(IMG_DEV):
            image += (ids >= ends[i]).astype(jnp.int32)
        return image

    def mod_rows(which, image):
        out = jnp.zeros((image.shape[0], width), F32)
        for i in range(IMG_DEV):
            row = modf[pl.ds(which * IMG_DEV + i, 1), :]
            out = jnp.where(image == i, row, out)
        return out

    mask = mask_ref[...].astype(F32)
    upper = jnp.where(
        lax.broadcasted_iota(jnp.int32, (128, 128), 0)
        <= lax.broadcasted_iota(jnp.int32, (128, 128), 1),
        1.0,
        0.0,
    ).astype(BF16)
    within = mm(mask.astype(BF16), upper)
    before = jnp.zeros((1, 1), F32)
    for i in range(toks // 128):
        row = within[i : i + 1, :]
        rank_row[:, i * 128 : (i + 1) * 128] = jnp.where(
            mask[i : i + 1, :] > 0.0, row + before - 1.0, -1.0
        ).astype(jnp.int32)
        before = before + row[:, 127:128]

    loads[0].wait()
    loads[1].wait()
    own_cols = pl.ds(pl.multiple_of(t * cols, 32), cols)

    def pick(b, carry):
        ids = lax.broadcasted_iota(jnp.int32, (128, toks), 0) + b * 128
        place = jnp.where(rank_row[...] == ids, 1.0, 0.0).astype(BF16)
        at = pl.ds(pl.multiple_of(b * 128, 128), 128)
        xg[own_cols, at] = mm_t(tok[...], place).astype(BF16)
        dyg[own_cols, at] = mm_t(dyt[...], place).astype(BF16)
        return carry

    lax.fori_loop(0, ROWS // 128, pick, 0)

    pl.semaphore_wait(barrier, 3 + n_seq - 1)

    def col_slot(buf):
        return lambda d: buf.at[pl.ds(pl.multiple_of(d * cols, 32), cols)]

    def row_slot(buf):
        return lambda d: buf.at[pl.ds(pl.multiple_of(d * PART, PART), PART)]

    def gather_start(slot, base):
        sent.append(send(slot(t), slot(t), "ag", base, {"tp": far}))
        sent.append(send(slot(t), slot(t), "ag", base + 1, {"tp": sib}))

    def gather_pass(slot, base):
        got(slot(far), "ag", base, {"tp": far})
        sent.append(send(slot(far), slot(far), "ag", base + 2, {"tp": sib}))

    def gather_end(slot, base):
        got(slot(sib), "ag", base + 1, {"tp": sib})
        got(slot(diag), "ag", base + 2, {"tp": sib})

    gather_start(col_slot(xg), 0)
    act_all = jax.nn.silu(cond_ref[...]).astype(BF16)
    pick_images = jnp.where(
        lax.broadcasted_iota(jnp.int32, (8, images), 1)
        == lax.broadcasted_iota(jnp.int32, (8, images), 0) + seq * IMG_DEV,
        1.0,
        0.0,
    ).astype(BF16)
    act_own = mm(pick_images, act_all).astype(BF16)
    modr[t, 24:32, :] = jnp.zeros((8, cols), F32)
    modr[t, 24:25, :] = bias_ref[8:9, :]
    modr[t, 25:26, :] = bias_ref[9:10, :]
    for j in range(6):
        ada_copies[j].wait()
        vectors = mm_t(act_own, ada_spots[j][...]) + bias_ref[j : j + 1, :]
        modr[t, j * IMG_DEV : (j + 1) * IMG_DEV, :] = vectors[0:IMG_DEV]
    for k in range(1, 4):
        to = (t + k) % 4
        sent.append(send(modr.at[t], modr.at[t], "mod", k - 1, {"tp": to}))
    gather_start(col_slot(dyg), 3)
    gather_pass(col_slot(xg), 0)
    for k in range(1, 4):
        source = (t + 4 - k) % 4
        got(modr.at[source], "mod", k - 1, {"tp": source})
    for d in range(4):
        modf[:, d * cols : (d + 1) * cols] = modr[d]
    gather_end(col_slot(xg), 0)
    x_nat[...] = xg[...].T
    own = pl.ds(pl.multiple_of(t * PART, PART), PART)
    own_image = rows_image(t * PART, PART)
    x_own[...] = x_nat[own, :]

    def norm_one(b, carry):
        at = pl.ds(pl.multiple_of(b * PART, PART), PART)
        image = rows_image(b * PART, PART)
        normed, _ = norm_rows(x_nat[at, :].astype(F32))
        h1[at, :] = (normed * (1.0 + mod_rows(1, image)) + mod_rows(0, image)).astype(BF16)
        return carry

    lax.fori_loop(0, 4, norm_one, 0)
    gather_pass(col_slot(dyg), 3)

    loads[2].wait()
    qkv_bias = jnp.concatenate(
        [bias_ref[6:7, :], jnp.zeros((1, head_cols), F32), bias_ref[7:8, :]], axis=1
    )

    def project(b, carry):
        at = pl.ds(pl.multiple_of(b * 320, 320), 320)
        rows = (mm_t(h1[at, :], wqkv[...]) + qkv_bias).astype(BF16)
        for i in range(3 * heads):
            qkvh[i, at, :] = rows[:, i * HEAD_DIM : (i + 1) * HEAD_DIM]
        return carry

    lax.fori_loop(0, 2, project, 0)

    image_row = jnp.zeros((1, ROWS), jnp.int32)
    row_ids = lax.broadcasted_iota(jnp.int32, (1, ROWS), 1)
    for i in range(IMG_DEV):
        image_row += (row_ids >= ends[i]).astype(jnp.int32)

    windows = []
    for b in range(4):
        first = max(0, (b * PART - KEEP_MOST + 1) // 128 * 128)
        last = min(ROWS, -(-((b + 1) * PART + KEEP_MOST - 1) // 128) * 128)
        windows.append((slice(b * PART, (b + 1) * PART), slice(first, last)))

    def attend(hd, carry):
        for b, (at, keys) in enumerate(windows):
            scores = mm_t(qkvh[hd, at, :], qkvh[heads + hd, keys, :]) * scale
            masked = jnp.where(
                rows_image(b * PART, PART) == image_row[:, keys], scores, -1e30
            )
            exps = jnp.exp(masked - jnp.max(masked, axis=1, keepdims=True))
            probs = (exps * (1.0 / jnp.sum(exps, axis=1, keepdims=True))).astype(BF16)
            pbs[hd, at, keys] = probs
            if keys.start > 0:
                pbs[hd, at, 0 : keys.start] = jnp.zeros((PART, keys.start), BF16)
            if keys.stop < ROWS:
                pbs[hd, at, keys.stop : ROWS] = jnp.zeros((PART, ROWS - keys.stop), BF16)
            oh[hd, at, :] = mm(probs, qkvh[2 * heads + hd, keys, :]).astype(BF16)
        return carry

    lax.fori_loop(0, heads, attend, 0)
    for hd in range(heads):
        oc[:, hd * HEAD_DIM : (hd + 1) * HEAD_DIM] = oh[hd]

    def store_blocks(buf, tile_at, values):
        low = values.astype(BF16)
        for b in range(4):
            buf[b % 2, b // 2, :, tile_at] = low[b * PART : (b + 1) * PART]

    def scatter_start(buf, first, base):
        sent.append(send(buf.at[1 - l, 1 - h], first.at[1 - h], "rs", base, {"tp": sib}))
        sent.append(send(buf.at[1 - l, h], first.at[h], "rs", base + 1, {"tp": sib}))

    def scatter_pass(buf, first, mid, second, base):
        got(first.at[1 - h], "rs", base, {"tp": sib})
        mid[...] = (buf[l, 1 - h].astype(F32) + first[1 - h].astype(F32)).astype(BF16)
        sent.append(send(mid, second, "rs", base + 2, {"tp": far}))

    def scatter_end(buf, first, second, base):
        got(first.at[h], "rs", base + 1, {"tp": sib})
        got(second, "rs", base + 2, {"tp": far})
        return (
            buf[l, h].astype(F32) + first[h].astype(F32) + second[...].astype(F32)
        )

    def tile(j):
        return pl.ds(pl.multiple_of(j * TILE, TILE), TILE)

    loads[3].wait()

    def branch_one(j, carry):
        store_blocks(rsb, tile(j), mm(oc[...], wproj[:, tile(j)]))
        return carry

    lax.fori_loop(0, width // TILE, branch_one, 0)
    scatter_start(rsb, rv1, 0)
    scatter_pass(rsb, rv1, sd2, rv2, 0)
    gather_end(col_slot(dyg), 3)

    dy_nat[...] = dyg[...].T
    dy_own[...] = dy_nat[own, :].astype(F32)

    def out_cotangent(b, carry):
        at = pl.ds(pl.multiple_of(b * PART, PART), PART)
        image = rows_image(b * PART, PART)
        dm[at, :] = (dy_nat[at, :].astype(F32) * mod_rows(5, image)).astype(BF16)
        return carry

    lax.fori_loop(0, 4, out_cotangent, 0)
    h1t[...] = h1[...].T

    attn_out = scatter_end(rsb, rv1, rv2, 0) + modf[24:25, :]
    a_own[...] = attn_out
    middle = x_own[...].astype(F32) + mod_rows(2, own_image) * attn_out
    x1_own[...] = middle
    normed_two, inverse_two = norm_rows(middle.astype(BF16).astype(F32))
    n2_own[...] = normed_two
    ag[own, :] = (normed_two * (1.0 + mod_rows(4, own_image)) + mod_rows(3, own_image)).astype(
        BF16
    )
    gather_start(row_slot(ag), 6)
    own_slice = jnp.where(
        lax.broadcasted_iota(jnp.int32, (width, slice_width), 0)
        == lax.broadcasted_iota(jnp.int32, (width, slice_width), 1) + seq * slice_width,
        1.0,
        0.0,
    ).astype(BF16)
    slice_sel[...] = own_slice
    cond_cols = sum(mm(part, own_slice) for part in parts_of(cond_ref[...], 3))
    sigmoid = jax.nn.sigmoid(cond_cols)
    slope_cols[...] = sigmoid * (1.0 + cond_cols * (1.0 - sigmoid))
    act_cols[...] = mm(jax.nn.silu(cond_ref[...]).astype(BF16), own_slice).astype(BF16)
    label_hot[...] = jnp.where(
        lax.broadcasted_iota(jnp.int32, (classes, images), 0) == labels_ref[...], 1.0, 0.0
    ).astype(BF16)
    dmt[...] = dm[...].T
    gather_pass(row_slot(ag), 6)
    loads[4].wait()
    loads[5].wait()
    gather_end(row_slot(ag), 6)

    hid_bias = jnp.concatenate([bias_ref[10 + d : 11 + d, :] for d in range(4)], axis=1)

    for j in range(ff // TILE):
        at = slice(j * TILE, (j + 1) * TILE)
        act, slope = gelu_pair(mm(ag[...], whid[:, at]) + hid_bias[:, at])
        g_act[:, at] = act.astype(BF16)
        du[:, at] = (slope * mm_t(dm[...], wout[at, :])).astype(BF16)

    finish_sends()

    def two_back(j, carry):
        store_blocks(rsb, tile(j), mm_t(du[...], whid[tile(j), :]))
        return carry

    lax.fori_loop(0, width // TILE, two_back, 0)
    h2t[...] = ag[...].T
    scatter_start(rsb, rv1, 3)

    def unit_bits(unit):
        return (1, 0) if reduce_here and unit in Z_FIRST else (0, 1)

    def unit_peer(bit):
        return {"seq": seq + (1 - 2 * bits[bit]) * (1 << bit)}

    def put_unit(unit, values, at):
        low = values.astype(BF16)
        step = width // BLOCKS
        first, second = unit_bits(unit)
        for j in range(BLOCKS):
            units[unit % SLOTS, (j >> first) & 1, (j >> second) & 1, j >> 2, :, at] = low[
                j * step : (j + 1) * step
            ]

    def unit_free(unit):
        if reduce_here:
            y_copies.pop(unit).wait_send()
            for copy in z_copies.pop(unit):
                copy.wait_send()
        else:
            y_copies.pop(unit).wait()

    def unit_send(unit):
        slot = unit % SLOTS
        if reduce_here:
            first = unit_bits(unit)[0]
            y_copies[unit] = send(
                units.at[slot, 1 - bits[first]], ry.at[unit], "y", unit, unit_peer(first)
            )
            z_copies[unit] = []
        else:
            copy = pltpu.make_async_copy(units.at[slot], parts_hbm.at[unit], y_s.at[unit])
            copy.start()
            y_copies[unit] = copy

    split = 3 * head_cols - 2 * TILE

    def unit_pieces(unit):
        if unit < 3:
            return [(outg_ref.at[:, unit * TILE : (unit + 1) * TILE], 0, TILE)]
        if unit < 6:
            return [(hidg_ref.at[:, (unit - 3) * TILE : (unit - 2) * TILE], 0, TILE)]
        pieces = []
        for part in range(3):
            start = max((unit - 6) * TILE, part * head_cols)
            stop = min((unit - 5) * TILE, (part + 1) * head_cols)
            if start < stop:
                base = part * head_cols
                pieces.append(
                    (
                        qkvg_ref.at[part, :, start - base : stop - base],
                        start - (unit - 6) * TILE,
                        stop - (unit - 6) * TILE,
                    )
                )
        if unit == 8:
            pieces.append((projg_ref, split, TILE))
        return pieces

    def unit_near(unit):
        slot = unit % SLOTS
        first, second = unit_bits(unit)
        mine, other = bits[first], 1 - bits[second]
        got(ry.at[unit], "y", unit, unit_peer(first))
        units[slot, mine, other] = (
            units[slot, mine, other].astype(F32) + ry[unit, other].astype(F32)
        ).astype(BF16)
        z_copies[unit].append(
            send(
                units.at[slot, mine, other], rz.at[unit, 0:2], "z", (unit, 0),
                unit_peer(second),
            )
        )

    def unit_far(unit):
        slot = unit % SLOTS
        first, second = unit_bits(unit)
        mine, same, last = bits[first], bits[second], bits[2]
        got(rz.at[unit, 0:2], "z", (unit, 0), unit_peer(second))

        def summed(which):
            return (
                units[slot, mine, same, which].astype(F32)
                + ry[unit, same, which].astype(F32)
                + rz[unit, which].astype(F32)
            )

        units[slot, mine, same, 1 - last] = summed(1 - last).astype(BF16)
        z_copies[unit].append(
            send(
                units.at[slot, mine, same, 1 - last], rz.at[unit, 2], "z", (unit, 1),
                unit_peer(2),
            )
        )
        total = summed(last)
        for ref, start, stop in unit_pieces(unit):
            ref[...] = total[:, start:stop]

    def unit_end(unit):
        got(rz.at[unit, 2], "z", (unit, 1), unit_peer(2))
        total = rz[unit, 2].astype(F32)
        for ref, start, stop in unit_pieces(unit):
            ref[...] = ref[...] + total[:, start:stop]

    def advance(*stages):
        if reduce_here:
            for stage, unit in stages:
                stage(unit)

    near, far_step, end = unit_near, unit_far, unit_end

    put_unit(0, mm(dmt[...], g_act[:, 0:TILE]), slice(None))
    unit_send(0)
    scatter_pass(rsb, rv1, sd2, rv2, 3)
    for j in range(1, 3):
        put_unit(j, mm(dmt[...], g_act[:, j * TILE : (j + 1) * TILE]), slice(None))
        unit_send(j)
    for j in range(3):
        put_unit(3 + j, mm(h2t[...], du[:, j * TILE : (j + 1) * TILE]), slice(None))
        unit_send(3 + j)

    def segments(which, values):
        for i in range(IMG_DEV):
            smp[which * IMG_DEV + i : which * IMG_DEV + i + 1, :] = jnp.sum(
                jnp.where(own_image == i, values, 0.0), axis=0, keepdims=True
            )

    smp[24:32, :] = jnp.zeros((8, width), F32)
    own_grad = scatter_end(rsb, rv1, rv2, 3)
    middle_grad = dy_own[...] + norm_pull(
        n2_own[...], inverse_two, own_grad * (1.0 + mod_rows(4, own_image))
    )
    attn_grad = (middle_grad * mod_rows(2, own_image)).astype(BF16)
    ag[own, :] = attn_grad
    gather_start(row_slot(ag), 9)
    dx1_own[...] = middle_grad
    segments(3, own_grad)
    segments(4, own_grad * n2_own[...])
    segments(2, middle_grad * a_own[...])
    smp[24:25, :] = jnp.sum(attn_grad.astype(F32), axis=0, keepdims=True)
    smp[25:26, :] = jnp.sum(
        (dy_own[...] * mod_rows(5, own_image)).astype(BF16).astype(F32), axis=0, keepdims=True
    )

    def branch_two(j, carry):
        store_blocks(msb, tile(j), mm(g_act[...], wout[:, tile(j)]))
        return carry

    lax.fori_loop(0, width // TILE, branch_two, 0)
    scatter_start(msb, mv1, 6)
    advance((near, 0), (near, 3), (far_step, 0))
    gather_pass(row_slot(ag), 9)
    scatter_pass(msb, mv1, md2, mv2, 6)
    advance((near, 1), (end, 0))
    gather_end(row_slot(ag), 9)

    def back_heads(b, carry):
        at = pl.ds(pl.multiple_of(b * PART, PART), PART)
        rows = mm_t(ag[at, :], wproj[...]).astype(BF16)
        for hd in range(heads):
            doh[hd, at, :] = rows[:, hd * HEAD_DIM : (hd + 1) * HEAD_DIM]
        return carry

    lax.fori_loop(0, 4, back_heads, 0)
    dsb[0:ROWS, :] = jnp.zeros((ROWS, ROWS), BF16)

    def attend_back(hd, carry):
        for at, keys in windows:
            probs = pbs[hd, at, keys].astype(F32)
            prob_grad = mm_t(doh[hd, at, :], qkvh[2 * heads + hd, keys, :])
            row_dot = jnp.sum(probs * prob_grad, axis=1, keepdims=True)
            score_grad = (probs * (prob_grad - row_dot)).astype(BF16)
            dsb[at, keys] = score_grad
            oh[hd, at, :] = (mm(score_grad, qkvh[heads + hd, keys, :]) * scale).astype(BF16)
        qkvh[heads + hd] = (t_mm(qkvh[hd], dsb[0:ROWS, :]) * scale).T.astype(BF16)
        qkvh[2 * heads + hd] = t_mm(doh[hd], pbs[hd]).T.astype(BF16)
        return carry

    lax.fori_loop(0, heads // 2, attend_back, 0)
    advance((far_step, 1), (near, 2))
    lax.fori_loop(heads // 2, heads, attend_back, 0)
    for i in range(3 * heads):
        dqkv[:, i * HEAD_DIM : (i + 1) * HEAD_DIM] = oh[i] if i < heads else qkvh[i]
    finish_sends()

    def one_back(j, carry):
        store_blocks(rsb, tile(j), mm(dqkv[...], wqkv[:, tile(j)]))
        return carry

    lax.fori_loop(0, width // TILE, one_back, 0)
    scatter_start(rsb, rv1, 9)
    h2t[...] = ag[...].T
    scatter_pass(rsb, rv1, sd2, rv2, 9)
    advance((end, 1), (far_step, 2), (near, 4))

    mlp_out = scatter_end(msb, mv1, mv2, 6) + modf[25:26, :]
    segments(5, dy_own[...] * mlp_out)
    final = (x1_own[...] + mod_rows(5, own_image) * mlp_out).astype(BF16)

    def columns_start(rows, base, which):
        for d in range(4):
            fin_out[which, d] = rows[:, d * cols : (d + 1) * cols]
        fin_in[which, t] = fin_out[which, t]
        for k in range(1, 4):
            to = (t + k) % 4
            sent.append(
                send(
                    fin_out.at[which, to], fin_in.at[which, t], "fin", base + k - 1,
                    {"tp": to},
                )
            )

    def columns_end(base, which):
        for k in range(1, 4):
            source = (t + 4 - k) % 4
            got(fin_in.at[which, source], "fin", base + k - 1, {"tp": source})
        return jnp.concatenate([fin_in[which, d] for d in range(4)], axis=0).T

    def place_back(rows_t, initial):
        def one(b, carry):
            at = pl.ds(pl.multiple_of(b * 256, 256), 256)
            rank = rank_row[:, at]
            ids = lax.broadcasted_iota(jnp.int32, (ROWS, 256), 0)
            place = jnp.where(rank == ids, 1.0, 0.0).astype(BF16)
            placed = mm(rows_t, place)
            initial[:, at] = jnp.where(rank >= 0, placed, initial[:, at].astype(F32)).astype(
                BF16
            )
            return carry

        lax.fori_loop(0, toks // 256, one, 0)

    columns_start(final, 0, 0)

    for j in range(2):
        unit_free(j)
        put_unit(6 + j, mm(h1t[...], dqkv[:, j * TILE : (j + 1) * TILE]), slice(None))
        unit_send(6 + j)
    unit_free(2)
    put_unit(8, mm(h1t[...], dqkv[:, 2 * TILE :]), slice(0, split))
    put_unit(8, mm(h2t[...], oc[...]), slice(split, TILE))
    unit_send(8)
    advance((end, 2), (far_step, 4))

    own_grad = scatter_end(rsb, rv1, rv2, 9)
    normed_one, inverse_one = norm_rows(x_own[...].astype(F32))
    in_grad = dx1_own[...] + norm_pull(
        normed_one, inverse_one, own_grad * (1.0 + mod_rows(1, own_image))
    )
    columns_start(in_grad.astype(BF16), 3, 1)
    advance((near, 5), (end, 4))
    segments(0, own_grad)
    segments(1, own_grad * normed_one)
    for d in range(4):
        sms[d] = smp[:, d * cols : (d + 1) * cols]
    for k in range(1, 4):
        to = (t + k) % 4
        sent.append(send(sms.at[to], smr.at[t], "sm", k - 1, {"tp": to}))
    qkv_sum = jnp.sum(dqkv[...].astype(F32), axis=0, keepdims=True)
    hid_sum = jnp.sum(du[...].astype(F32), axis=0, keepdims=True)
    place_back(columns_end(0, 0), tok)
    out_copy = pltpu.make_async_copy(tok, output_hbm, out_sem.at[0])
    out_copy.start()
    ada_copies = ada_loads()
    advance((near, 7), (far_step, 5), (far_step, 3))
    total = sms[t]
    for k in range(1, 4):
        source = (t + 4 - k) % 4
        got(smr.at[source], "sm", k - 1, {"tp": source})
        total += smr[source]
    sgr[seq] = total
    sgr[seq, 26:27, :] = qkv_sum[:, 0:head_cols]
    sgr[seq, 27:28, :] = qkv_sum[:, 2 * head_cols : 3 * head_cols]
    for d in range(4):
        sgr[seq, 28 + d : 29 + d, :] = hid_sum[:, d * cols : (d + 1) * cols]

    def tell(k, carry):
        pltpu.make_async_remote_copy(
            src_ref=sgr.at[seq], dst_ref=sgr.at[seq],
            send_sem=sg_s.at[k], recv_sem=sg_r.at[k],
            device_id={"seq": (seq + k) % n_seq}, device_id_type=MESH,
        ).start()
        return carry

    lax.fori_loop(1, n_seq, tell, 0)
    place_back(columns_end(3, 1), dyt)
    grad_copy = pltpu.make_async_copy(dyt, tokens_grad_hbm, out_sem.at[1])
    grad_copy.start()
    advance((near, 6), (end, 5), (end, 3))

    def hear(k, carry):
        source = (seq + n_seq - k) % n_seq
        copy = pltpu.make_async_remote_copy(
            src_ref=sgr.at[seq], dst_ref=sgr.at[source],
            send_sem=sg_s.at[k], recv_sem=sg_r.at[k],
            device_id={"seq": (seq + k) % n_seq}, device_id_type=MESH,
        )
        copy.wait_recv()
        copy.wait_send()
        return carry

    lax.fori_loop(1, n_seq, hear, 0)

    all_rows = n_seq * 32
    flat = parts_of(sgr[...].reshape(all_rows, cols), 2)
    row_id = lax.broadcasted_iota(jnp.int32, (all_rows, images), 0)
    image_id = lax.broadcasted_iota(jnp.int32, (all_rows, images), 1)
    base_image = (row_id >> 5) * IMG_DEV
    place_in = row_id & 31
    cond_part = jnp.zeros((images, width), F32)
    for j in range(6):
        rank_in = place_in - j * IMG_DEV
        member = jnp.where(
            (rank_in >= 0) & (rank_in < IMG_DEV) & (image_id == base_image + rank_in), 1.0, 0.0
        ).astype(BF16)
        found = [t_mm(member, part) for part in flat]
        vectors = [item.astype(BF16) for item in found]
        adag_ref[j] = sum(t_mm(act_cols[...], item) for item in vectors)
        adabg_ref[j : j + 1, :] = jnp.sum(sum(found), axis=0, keepdims=True)
        ada_copies[j].wait()
        cond_part += sum(mm(item, ada_spots[j][...]) for item in vectors)
        if j == 2:
            advance((near, 8), (far_step, 6))
    cgr[t] = sum(mm(item, slice_sel[...]) for item in parts_of(cond_part, 2))
    for k in range(1, 4):
        to = (t + k) % 4
        sent.append(send(cgr.at[t], cgr.at[t], "cg", k - 1, {"tp": to}))
    sums = jnp.sum(sgr[:, 24:32, :], axis=0)
    projbg_ref[...] = sums[0:1]
    outbg_ref[...] = sums[1:2]
    qvg_ref[...] = sums[2:4]
    for d in range(4):
        hidbg_ref[:, d * cols : (d + 1) * cols] = sums[4 + d : 5 + d]
    advance((far_step, 7), (far_step, 8))
    grads = cgr[t]
    for k in range(1, 4):
        source = (t + 4 - k) % 4
        got(cgr.at[source], "cg", k - 1, {"tp": source})
        grads += cgr[source]
    classg_ref[...] = sum(
        lax.dot_general(
            item, label_hot[...], (((0,), (1,)), ((), ())), preferred_element_type=F32
        )
        for item in parts_of(slope_cols[...] * grads, 2)
    )
    advance((end, 6), (end, 7), (end, 8))
    finish_sends()
    for unit in range(3, UNITS):
        unit_free(unit)
    out_copy.wait()
    grad_copy.wait()


def run_block(sizes, *operands):
    n_seq, width, cols, head_cols, ff, toks, images, classes = sizes
    heads = head_cols // HEAD_DIM
    reduce_here = n_seq == BLOCKS
    step = width // BLOCKS
    slice_width = width // n_seq
    vmem, dma = pltpu.VMEM, pltpu.SemaphoreType.DMA
    any_spec = pl.BlockSpec(memory_space=pl.ANY)
    vmem_spec = pl.BlockSpec(memory_space=pltpu.VMEM)

    def shaped(*shape):
        return jax.ShapeDtypeStruct(shape, F32)

    out_shape = [
        jax.ShapeDtypeStruct((cols, toks), BF16),
        jax.ShapeDtypeStruct((cols, toks), BF16),
        shaped(slice_width, classes),
        shaped(6, slice_width, cols),
        shaped(6, cols),
        shaped(2, cols),
        shaped(1, cols),
        shaped(1, cols),
        shaped(1, ff),
    ]
    out_specs = [any_spec, any_spec] + [vmem_spec] * 7
    if reduce_here:
        out_shape += [
            shaped(3, step, head_cols),
            shaped(step, head_cols),
            shaped(step, ff),
            shaped(step, ff),
        ]
        out_specs += [vmem_spec] * 4
    else:
        out_shape.append(jax.ShapeDtypeStruct((UNITS, 2, 2, 2, step, TILE), BF16))
        out_specs.append(any_spec)
    own = vmem((PART, width), F32)
    low = vmem((ROWS, width), BF16)
    high = vmem((width, ROWS), BF16)
    scratch = [
        vmem((cols, toks), BF16), vmem((cols, toks), BF16),
        vmem((3 * head_cols, width), BF16), vmem((head_cols, width), BF16),
        vmem((width, ff), BF16), vmem((ff, width), BF16), vmem((1, toks), jnp.int32),
        high, high,
        vmem((32, width), F32), low, high,
        vmem((3 * heads, ROWS, HEAD_DIM), BF16), vmem((heads, ROWS, ROWS), BF16),
        vmem((heads, ROWS, HEAD_DIM), BF16), vmem((ROWS, head_cols), BF16),
        vmem((2, 2, PART, width), BF16), vmem((2, PART, width), BF16),
        vmem((PART, width), BF16), vmem((PART, width), BF16),
        vmem((2, 2, PART, width), BF16), vmem((2, PART, width), BF16),
        vmem((PART, width), BF16), vmem((PART, width), BF16),
        low, high, low, high, vmem((ROWS, ff), BF16),
        vmem((heads, ROWS, HEAD_DIM), BF16), vmem((ROWS, 3 * head_cols), BF16),
        vmem((SLOTS, 2, 2, 2, step, TILE), BF16),
        vmem((UNITS if reduce_here else 1, 2, 2, step, TILE), BF16),
        vmem((UNITS if reduce_here else 1, BLOCKS // 2 - 1, step, TILE), BF16),
        vmem((2, 4, PART, cols), BF16), vmem((2, 4, PART, cols), BF16),
        vmem((PART, width), BF16), own, own, own, own, own,
        vmem((32, width), F32), vmem((4, 32, cols), F32), vmem((4, 32, cols), F32),
        vmem((4, 32, cols), F32), vmem((n_seq, 32, cols), F32),
        vmem((4, images, slice_width), F32), vmem((width, slice_width), BF16),
        vmem((images, slice_width), F32), vmem((images, slice_width), BF16),
        vmem((classes, images), BF16),
        dma((6,)), dma((6,)), dma((2,)),
        dma((12,)), dma((12,)), dma((12,)), dma((12,)), dma((3,)), dma((3,)),
        dma((6,)), dma((6,)), dma((3,)), dma((3,)), dma((3,)), dma((3,)),
        dma((n_seq,)), dma((n_seq,)),
        dma((UNITS,)), dma((UNITS,)), dma((UNITS, BLOCKS // 2 - 1)), dma((UNITS, BLOCKS // 2 - 1)),
    ]
    return pl.pallas_call(
        functools.partial(block_kernel, sizes),
        out_shape=out_shape,
        in_specs=[pl.BlockSpec(memory_space=pltpu.SMEM)] + [vmem_spec] * 4 + [any_spec] * 7,
        out_specs=out_specs,
        scratch_shapes=scratch,
        compiler_params=pltpu.CompilerParams(
            collective_id=0, has_side_effects=True, vmem_limit_bytes=63 * 1024 * 1024
        ),
    )(*operands)


def copy_kernel(count, *refs):
    sem = refs[3 * count]
    loads = [
        pltpu.make_async_copy(refs[i], refs[2 * count + i], sem.at[0, i]) for i in range(count)
    ]
    stores = [
        pltpu.make_async_copy(refs[2 * count + i], refs[count + i], sem.at[1, i])
        for i in range(count)
    ]
    for load in loads:
        load.start()
    for load, store in zip(loads, stores):
        load.wait()
        store.start()
    for store in stores:
        store.wait()


def copy_all(arrays):
    count = len(arrays)
    return pl.pallas_call(
        functools.partial(copy_kernel, count),
        out_shape=[jax.ShapeDtypeStruct(item.shape, item.dtype) for item in arrays],
        in_specs=[pl.BlockSpec(memory_space=pl.ANY)] * count,
        out_specs=[pl.BlockSpec(memory_space=pl.ANY)] * count,
        scratch_shapes=[pltpu.VMEM(item.shape, item.dtype) for item in arrays]
        + [pltpu.SemaphoreType.DMA((2, count))],
        compiler_params=pltpu.CompilerParams(vmem_limit_bytes=60 * 1024 * 1024),
    )(*arrays)


def time_embed(step_ids, model_width):
    half_width = model_width // 2
    frequency = jnp.exp(-math.log(10000.0) * jnp.arange(half_width, dtype=F32) / half_width)
    angles = step_ids.astype(F32)[:, None] * frequency[None, :]
    return jnp.concatenate([jnp.cos(angles), jnp.sin(angles)], axis=1)


def local(
    tokens,
    out_grad,
    route_mask,
    kept_counts,
    labels,
    timesteps,
    class_table,
    ada_weight,
    ada_bias,
    qkv_weight,
    qv_bias,
    proj_weight,
    proj_bias,
    hidden_weight,
    hidden_bias,
    output_weight,
    output_bias,
):
    n_seq = lax.axis_size("seq")
    toks, cols = tokens.shape
    classes, width = class_table.shape
    head_cols = qkv_weight.shape[2]
    ff = hidden_weight.shape[1]
    images = kept_counts.shape[0]

    label_hot = (labels[:, None] == jnp.arange(classes, dtype=jnp.int32)[None, :]).astype(BF16)
    condition = mm(label_hot, class_table) + time_embed(timesteps, width)
    biases = jnp.concatenate(
        [
            ada_bias,
            qv_bias,
            proj_bias[None],
            output_bias[None],
            hidden_bias.reshape(ff // cols, cols),
            jnp.zeros((2, cols), BF16),
        ]
    ).astype(F32)

    results = run_block(
        (n_seq, width, cols, head_cols, ff, toks, images, classes),
        kept_counts,
        route_mask.reshape(toks // 128, 128),
        condition,
        labels[None],
        biases,
        tokens.T,
        out_grad.T,
        ada_weight.transpose(1, 2, 0).reshape(6 * cols, width),
        qkv_weight.transpose(1, 2, 0).reshape(3 * head_cols, width),
        proj_weight,
        hidden_weight,
        output_weight,
    )
    results = list(copy_all(results if n_seq == BLOCKS else results[:9])) + list(results[9:])
    (
        output,
        tokens_grad,
        class_grad,
        ada_weight_grad,
        ada_bias_grad,
        qv_bias_grad,
        proj_bias_grad,
        output_bias_grad,
        hidden_bias_grad,
    ) = results[:9]
    if n_seq == BLOCKS:
        qkv_weight_grad, proj_weight_grad, hidden_weight_grad, output_weight_grad = results[9:13]
        qkv_weight_grad = qkv_weight_grad.transpose(1, 0, 2)
    else:
        parts = results[9].transpose(3, 2, 1, 4, 0, 5).reshape(width, UNITS * TILE)
        summed = lax.psum_scatter(parts, "seq", scatter_dimension=0, tiled=True).astype(F32)
        output_weight_grad = summed[:, :ff]
        hidden_weight_grad = summed[:, ff : 2 * ff]
        qkv_weight_grad = summed[:, 2 * ff : 2 * ff + 3 * head_cols].reshape(-1, 3, head_cols)
        proj_weight_grad = summed[:, 2 * ff + 3 * head_cols :]
    return (
        output.T,
        tokens_grad.T,
        class_grad.T,
        ada_weight_grad.transpose(1, 0, 2),
        ada_bias_grad,
        qkv_weight_grad,
        qv_bias_grad,
        proj_weight_grad.T,
        proj_bias_grad.reshape(cols),
        hidden_weight_grad,
        hidden_bias_grad.reshape(ff),
        output_weight_grad.T,
        output_bias_grad.reshape(cols),
    )


def solution(mesh):
    return jax.shard_map(
        local,
        mesh=mesh,
        in_specs=(
            P("seq", "tp"),
            P("seq", "tp"),
            P("seq"),
            P(),
            P(),
            P(),
            P(),
            P(None, None, "tp"),
            P(None, "tp"),
            P(None, None, "tp"),
            P(None, "tp"),
            P("tp", None),
            P("tp"),
            P(None, "tp"),
            P("tp"),
            P("tp", None),
            P("tp"),
        ),
        out_specs=(
            P("seq", "tp"),
            P("seq", "tp"),
            P(None, "seq"),
            P("seq", None, "tp"),
            P(None, "tp"),
            P("seq", None, "tp"),
            P(None, "tp"),
            P("tp", "seq"),
            P("tp"),
            P("seq", "tp"),
            P("tp"),
            P("tp", "seq"),
            P("tp"),
        ),
        check_vma=False,
    )
```

```python
import functools
import math

import jax
import jax.numpy as jnp
from jax import lax
from jax.experimental import pallas as pl
from jax.experimental.pallas import tpu as pltpu
from jax.sharding import PartitionSpec as P

HEAD_DIM = 72
IMG_DEV = 4
KEEP_MOST = 192
ROWS = 640
PART = 160
TILE = 384
UNITS = 9
SLOTS = 6
Z_FIRST = (3, 7)
BLOCKS = 8
NORM_EPS = 1e-06
HIGHEST = lax.Precision.HIGHEST
MESH = pl.DeviceIdType.MESH
F32 = jnp.float32
BF16 = jnp.bfloat16


def mm(left, right):
    return jnp.dot(left, right, preferred_element_type=F32)


def mm_t(left, right):
    return lax.dot_general(left, right, (((1,), (1,)), ((), ())), preferred_element_type=F32)


def t_mm(left, right):
    return lax.dot_general(left, right, (((0,), (0,)), ((), ())), preferred_element_type=F32)


def parts_of(values, count):
    parts = []
    for _ in range(count):
        part = values.astype(BF16)
        parts.append(part)
        values = values - part.astype(F32)
    return parts


def norm_rows(values):
    centered = values - jnp.mean(values, axis=1, keepdims=True)
    inverse = lax.rsqrt(jnp.mean(centered * centered, axis=1, keepdims=True) + NORM_EPS)
    return centered * inverse, inverse


def norm_pull(normed, inverse, grad):
    return inverse * (
        grad
        - jnp.mean(grad, axis=1, keepdims=True)
        - normed * jnp.mean(grad * normed, axis=1, keepdims=True)
    )


def gelu_pair(values):
    coef = math.sqrt(2.0 / math.pi)
    square = values * values
    tanh = jnp.tanh(coef * (values + 0.044715 * (values * square)))
    half = 0.5 * (1.0 + tanh)
    slope = half + 0.5 * values * (1.0 - tanh * tanh) * (
        coef * (1.0 + (3.0 * 0.044715) * square)
    )
    return values * half, slope


def block_kernel(
    sizes,
    counts_ref,
    mask_ref,
    cond_ref,
    labels_ref,
    ada_bias_ref,
    qv_bias_ref,
    bias_ref,
    tokens_hbm,
    grad_hbm,
    ada_hbm,
    wqkv_hbm,
    wproj_hbm,
    whid_hbm,
    wout_hbm,
    output_hbm,
    tokens_grad_hbm,
    classg_ref,
    adag_ref,
    adabg_ref,
    qvg_ref,
    projbg_ref,
    outbg_ref,
    hidbg_ref,
    *rest,
):
    n_seq, width, cols, head_cols, ff, toks, images, classes = sizes
    reduce_here = n_seq == BLOCKS
    slice_width = width // n_seq
    if reduce_here:
        qkvg_ref, projg_ref, hidg_ref, outg_ref = rest[:4]
        rest = rest[4:]
    else:
        parts_hbm = rest[0]
        rest = rest[1:]
    (
        tok, dyt, wqkv, wproj, whid, wout, rank_row, image_lane,
        xg, dyg, modf, h1, h1t, qkvh, pbs, oh, oc, rsb, rv1, sd2, rv2,
        msb, mv1, md2, mv2, ag, h2t, dm, dmt, du, doh, dqkv,
        units, ry, rz, fin_in, fin_out, x_own, a_own, x1_own, n2_own, dx1_own, dy_own,
        smp, sms, smr, modr, sgr, cgr, slice_sel, slope_cols, act_cols, label_hot,
        in_sem, ada_sem, out_sem,
        ag_s, ag_r, rs_s, rs_r, mod_s, mod_r, fin_s, fin_r, sm_s, sm_r, cg_s, cg_r, sg_s, sg_r,
        y_s, y_r, z_s, z_r,
    ) = rest
    heads = head_cols // HEAD_DIM
    scale = HEAD_DIM ** (-0.5)
    g_act = h1
    x_nat = h1
    dy_nat = dm
    dsb = dmt

    seq = lax.axis_index("seq")
    t = lax.axis_index("tp")
    h, l = t // 2, t % 2
    bits = (seq % 2, (seq // 2) % 2, (seq // 4) % 2)
    sib = t + 1 - 2 * l
    far = t + 2 - 4 * h
    diag = 3 - t

    sems = {
        "ag": (ag_s, ag_r), "rs": (rs_s, rs_r), "mod": (mod_s, mod_r), "fin": (fin_s, fin_r),
        "sm": (sm_s, sm_r), "y": (y_s, y_r), "z": (z_s, z_r), "cg": (cg_s, cg_r),
    }

    def remote(src, dst, kind, index, where):
        ssem, rsem = sems[kind]
        return pltpu.make_async_remote_copy(
            src_ref=src, dst_ref=dst, send_sem=ssem.at[index], recv_sem=rsem.at[index],
            device_id=where, device_id_type=MESH,
        )

    def send(src, dst, kind, index, where):
        copy = remote(src, dst, kind, index, where)
        copy.start()
        return copy

    def got(dst, kind, index, where):
        remote(dst, dst, kind, index, where).wait_recv()

    sent = []
    y_copies = {}
    z_copies = {}

    def finish_sends():
        for copy in sent:
            copy.wait_send()
        sent.clear()

    barrier = pltpu.get_barrier_semaphore()
    for k in range(1, 4):
        pl.semaphore_signal(
            barrier, inc=1, device_id={"tp": (t + k) % 4}, device_id_type=MESH
        )

    def greet(k, carry):
        pl.semaphore_signal(
            barrier, inc=1, device_id={"seq": (seq + k) % n_seq}, device_id_type=MESH
        )
        return carry

    lax.fori_loop(1, n_seq, greet, 0)

    ada_spots = [
        buf.at[pl.ds(part * cols, cols)] for buf in (dm, du, h1) for part in range(2)
    ]

    def ada_loads():
        copies = [
            pltpu.make_async_copy(
                ada_hbm.at[pl.ds(j * cols, cols)], ada_spots[j], ada_sem.at[j]
            )
            for j in range(6)
        ]
        for copy in copies:
            copy.start()
        return copies

    loads = [
        pltpu.make_async_copy(src, dst, in_sem.at[i])
        for i, (src, dst) in enumerate(
            [
                (tokens_hbm, tok), (grad_hbm, dyt), (wqkv_hbm, wqkv),
                (wproj_hbm, wproj), (whid_hbm, whid), (wout_hbm, wout),
            ]
        )
    ]
    loads[0].start()
    loads[1].start()
    ada_copies = ada_loads()
    for load in loads[2:]:
        load.start()

    ends = []
    for i in range(IMG_DEV):
        count = counts_ref[seq * IMG_DEV + i]
        ends.append(count if i == 0 else ends[-1] + count)

    def rows_image(start, count):
        ids = lax.broadcasted_iota(jnp.int32, (count, 1), 0) + start
        image = jnp.zeros((count, 1), jnp.int32)
        for i in range(IMG_DEV):
            image += (ids >= ends[i]).astype(jnp.int32)
        return image

    def mod_rows(which, image):
        out = jnp.zeros((image.shape[0], width), F32)
        for i in range(IMG_DEV):
            row = modf[pl.ds(which * IMG_DEV + i, 1), :]
            out = jnp.where(image == i, row, out)
        return out

    mask = mask_ref[...].astype(F32)
    upper = jnp.where(
        lax.broadcasted_iota(jnp.int32, (128, 128), 0)
        <= lax.broadcasted_iota(jnp.int32, (128, 128), 1),
        1.0,
        0.0,
    ).astype(BF16)
    within = mm(mask.astype(BF16), upper)
    before = jnp.zeros((1, 1), F32)
    for i in range(toks // 128):
        row = within[i : i + 1, :]
        rank_row[:, i * 128 : (i + 1) * 128] = jnp.where(
            mask[i : i + 1, :] > 0.0, row + before - 1.0, -1.0
        ).astype(jnp.int32)
        before = before + row[:, 127:128]

    own_cols = pl.ds(pl.multiple_of(t * cols, 32), cols)

    def pick(source, target):
        def one(b, carry):
            ids = lax.broadcasted_iota(jnp.int32, (128, toks), 0) + b * 128
            place = jnp.where(rank_row[...] == ids, 1.0, 0.0).astype(BF16)
            at = pl.ds(pl.multiple_of(b * 128, 128), 128)
            target[own_cols, at] = mm_t(source[...], place).astype(BF16)
            return carry

        lax.fori_loop(0, ROWS // 128, one, 0)

    loads[0].wait()
    pick(tok, xg)

    pl.semaphore_wait(barrier, 3 + n_seq - 1)

    def col_slot(buf):
        return lambda d: buf.at[pl.ds(pl.multiple_of(d * cols, 32), cols)]

    def row_slot(buf):
        return lambda d: buf.at[pl.ds(pl.multiple_of(d * PART, PART), PART)]

    def gather_start(slot, base):
        sent.append(send(slot(t), slot(t), "ag", base, {"tp": far}))
        sent.append(send(slot(t), slot(t), "ag", base + 1, {"tp": sib}))

    def gather_pass(slot, base):
        got(slot(far), "ag", base, {"tp": far})
        sent.append(send(slot(far), slot(far), "ag", base + 2, {"tp": sib}))

    def gather_near(slot, base):
        got(slot(sib), "ag", base + 1, {"tp": sib})

    def gather_last(slot, base):
        got(slot(diag), "ag", base + 2, {"tp": sib})

    def gather_end(slot, base):
        gather_near(slot, base)
        gather_last(slot, base)

    gather_start(col_slot(xg), 0)
    loads[1].wait()
    pick(dyt, dyg)
    act_all = jax.nn.silu(cond_ref[...]).astype(BF16)
    pick_images = jnp.where(
        lax.broadcasted_iota(jnp.int32, (8, images), 1)
        == lax.broadcasted_iota(jnp.int32, (8, images), 0) + seq * IMG_DEV,
        1.0,
        0.0,
    ).astype(BF16)
    act_own = mm(pick_images, act_all).astype(BF16)
    modr[t, 24:32, :] = jnp.zeros((8, cols), F32)
    ada_bias = ada_bias_ref[...].astype(F32)
    qv_bias = qv_bias_ref[...].astype(F32)
    modr[t, 24:25, :] = bias_ref[0:1, :]
    modr[t, 25:26, :] = bias_ref[1:2, :]
    for j in range(6):
        ada_copies[j].wait()
        vectors = mm_t(act_own, ada_spots[j][...]) + ada_bias[j : j + 1]
        modr[t, j * IMG_DEV : (j + 1) * IMG_DEV, :] = vectors[0:IMG_DEV]
    for k in range(1, 4):
        to = (t + k) % 4
        sent.append(send(modr.at[t], modr.at[t], "mod", k - 1, {"tp": to}))
    gather_start(col_slot(dyg), 3)
    gather_pass(col_slot(xg), 0)
    for k in range(1, 4):
        source = (t + 4 - k) % 4
        got(modr.at[source], "mod", k - 1, {"tp": source})
    for d in range(4):
        modf[:, d * cols : (d + 1) * cols] = modr[d]
    gather_end(col_slot(xg), 0)
    x_nat[...] = xg[...].T
    own = pl.ds(pl.multiple_of(t * PART, PART), PART)
    own_image = rows_image(t * PART, PART)
    x_own[...] = x_nat[own, :]

    def norm_one(b, carry):
        at = pl.ds(pl.multiple_of(b * PART, PART), PART)
        image = rows_image(b * PART, PART)
        normed, _ = norm_rows(x_nat[at, :].astype(F32))
        h1[at, :] = (normed * (1.0 + mod_rows(1, image)) + mod_rows(0, image)).astype(BF16)
        return carry

    lax.fori_loop(0, 4, norm_one, 0)
    gather_pass(col_slot(dyg), 3)

    loads[2].wait()
    qkv_bias = jnp.concatenate(
        [qv_bias[0:1], jnp.zeros((1, head_cols), F32), qv_bias[1:2]], axis=1
    )

    def project(b, carry):
        at = pl.ds(pl.multiple_of(b * 320, 320), 320)
        rows = (mm_t(h1[at, :], wqkv[...]) + qkv_bias).astype(BF16)
        for i in range(3 * heads):
            qkvh[i, at, :] = rows[:, i * HEAD_DIM : (i + 1) * HEAD_DIM]
        return carry

    lax.fori_loop(0, 2, project, 0)

    image_row = jnp.zeros((1, ROWS), jnp.int32)
    row_ids = lax.broadcasted_iota(jnp.int32, (1, ROWS), 1)
    for i in range(IMG_DEV):
        image_row += (row_ids >= ends[i]).astype(jnp.int32)

    windows = []
    for b in range(4):
        first = max(0, (b * PART - KEEP_MOST + 1) // 128 * 128)
        last = min(ROWS, -(-((b + 1) * PART + KEEP_MOST - 1) // 128) * 128)
        windows.append((slice(b * PART, (b + 1) * PART), slice(first, last)))

    image_lane[...] = image_row

    def attend_block(b):
        at = pl.ds(pl.multiple_of(b * PART, PART), PART)
        span = 512
        upper_half = b // 2
        keys = pl.ds(pl.multiple_of(upper_half * (ROWS - span), 128), span)
        unused = pl.ds(pl.multiple_of((1 - upper_half) * span, 128), ROWS - span)

        def one(hd, carry):
            scores = mm_t(qkvh[hd, at, :], qkvh[heads + hd, keys, :]) * scale
            masked = jnp.where(
                rows_image(b * PART, PART) == image_lane[:, keys], scores, -1e30
            )
            exps = jnp.exp(masked - jnp.max(masked, axis=1, keepdims=True))
            probs = (exps * (1.0 / jnp.sum(exps, axis=1, keepdims=True))).astype(BF16)
            pbs[hd, at, keys] = probs
            pbs[hd, at, unused] = jnp.zeros((PART, ROWS - span), BF16)
            oh[hd, at, :] = mm(probs, qkvh[2 * heads + hd, keys, :]).astype(BF16)
            return carry

        lax.fori_loop(0, heads, one, 0)
        for hd in range(heads):
            oc[at, hd * HEAD_DIM : (hd + 1) * HEAD_DIM] = oh[hd, at, :]
        rsb[b % 2, b // 2] = mm(oc[at, :], wproj[...]).astype(BF16)

    def store_blocks(buf, tile_at, values):
        low = values.astype(BF16)
        for b in range(4):
            buf[b % 2, b // 2, :, tile_at] = low[b * PART : (b + 1) * PART]

    def scatter_first(buf, first, half, base):
        sent.append(send(buf.at[1 - l, half], first.at[half], "rs", base, {"tp": sib}))

    def scatter_start(buf, first, base):
        scatter_first(buf, first, 1 - h, base)
        scatter_first(buf, first, h, base + 1)

    def scatter_halves(product, base):
        for step, half in ((0, 1 - h), (1, h)):
            rows = pl.ds(pl.multiple_of(half * 2 * PART, 2 * PART), 2 * PART)

            def one(j, carry):
                low = product(rows, tile(j)).astype(BF16)
                for b in range(2):
                    rsb[b, half, :, tile(j)] = low[b * PART : (b + 1) * PART]
                return carry

            lax.fori_loop(0, width // TILE, one, 0)
            scatter_first(rsb, rv1, half, base + step)
            if step == 1:
                scatter_pass(rsb, rv1, sd2, rv2, base)

    def scatter_pass(buf, first, mid, second, base):
        got(first.at[1 - h], "rs", base, {"tp": sib})
        mid[...] = (buf[l, 1 - h].astype(F32) + first[1 - h].astype(F32)).astype(BF16)
        sent.append(send(mid, second, "rs", base + 2, {"tp": far}))

    def scatter_end(buf, first, second, base):
        got(first.at[h], "rs", base + 1, {"tp": sib})
        got(second, "rs", base + 2, {"tp": far})
        return (
            buf[l, h].astype(F32) + first[h].astype(F32) + second[...].astype(F32)
        )

    def tile(j):
        return pl.ds(pl.multiple_of(j * TILE, TILE), TILE)

    loads[3].wait()
    attend_block(diag)
    scatter_first(rsb, rv1, 1 - h, 0)
    attend_block(far)
    scatter_pass(rsb, rv1, sd2, rv2, 0)
    attend_block(sib)
    scatter_first(rsb, rv1, h, 1)
    attend_block(t)
    gather_end(col_slot(dyg), 3)

    dy_nat[...] = dyg[...].T
    dy_own[...] = dy_nat[own, :].astype(F32)

    def out_cotangent(b, carry):
        at = pl.ds(pl.multiple_of(b * PART, PART), PART)
        image = rows_image(b * PART, PART)
        dm[at, :] = (dy_nat[at, :].astype(F32) * mod_rows(5, image)).astype(BF16)
        return carry

    lax.fori_loop(0, 4, out_cotangent, 0)
    h1t[...] = h1[...].T

    attn_out = scatter_end(rsb, rv1, rv2, 0) + modf[24:25, :]
    a_own[...] = attn_out
    middle = x_own[...].astype(F32) + mod_rows(2, own_image) * attn_out
    x1_own[...] = middle
    normed_two, inverse_two = norm_rows(middle.astype(BF16).astype(F32))
    n2_own[...] = normed_two
    ag[own, :] = (normed_two * (1.0 + mod_rows(4, own_image)) + mod_rows(3, own_image)).astype(
        BF16
    )
    gather_start(row_slot(ag), 6)
    own_slice = jnp.where(
        lax.broadcasted_iota(jnp.int32, (width, slice_width), 0)
        == lax.broadcasted_iota(jnp.int32, (width, slice_width), 1) + seq * slice_width,
        1.0,
        0.0,
    ).astype(BF16)
    slice_sel[...] = own_slice
    cond_cols = sum(mm(part, own_slice) for part in parts_of(cond_ref[...], 3))
    sigmoid = jax.nn.sigmoid(cond_cols)
    slope_cols[...] = sigmoid * (1.0 + cond_cols * (1.0 - sigmoid))
    act_cols[...] = mm(jax.nn.silu(cond_ref[...]).astype(BF16), own_slice).astype(BF16)
    label_hot[...] = jnp.where(
        lax.broadcasted_iota(jnp.int32, (classes, images), 0) == labels_ref[...], 1.0, 0.0
    ).astype(BF16)
    dmt[...] = dm[...].T
    loads[4].wait()
    loads[5].wait()
    hidbg_ref[...] = jnp.concatenate([bias_ref[2 + d : 3 + d, :] for d in range(4)], axis=1)

    def mlp(half):
        rows = pl.ds(pl.multiple_of(half * 2 * PART, 2 * PART), 2 * PART)

        def one(j, carry):
            at = tile(j)
            act, slope = gelu_pair(mm(ag[rows, :], whid[:, at]) + hidbg_ref[:, at])
            g_act[rows, at] = act.astype(BF16)
            du[rows, at] = (slope * mm_t(dm[rows, :], wout[at, :])).astype(BF16)
            return carry

        lax.fori_loop(0, ff // TILE, one, 0)

    gather_near(row_slot(ag), 6)
    mlp(h)
    gather_pass(row_slot(ag), 6)
    gather_last(row_slot(ag), 6)
    mlp(1 - h)

    finish_sends()

    def unit_bits(unit):
        return (1, 0) if reduce_here and unit in Z_FIRST else (0, 1)

    def unit_peer(bit):
        return {"seq": seq + (1 - 2 * bits[bit]) * (1 << bit)}

    def put_unit(unit, values, at):
        low = values.astype(BF16)
        step = width // BLOCKS
        first, second = unit_bits(unit)
        for j in range(BLOCKS):
            units[unit % SLOTS, (j >> first) & 1, (j >> second) & 1, j >> 2, :, at] = low[
                j * step : (j + 1) * step
            ]

    def unit_free(unit):
        if reduce_here:
            y_copies.pop(unit).wait_send()
            for copy in z_copies.pop(unit):
                copy.wait_send()
        else:
            y_copies.pop(unit).wait()

    def unit_send(unit):
        slot = unit % SLOTS
        if reduce_here:
            first = unit_bits(unit)[0]
            y_copies[unit] = send(
                units.at[slot, 1 - bits[first]], ry.at[unit], "y", unit, unit_peer(first)
            )
            z_copies[unit] = []
        else:
            copy = pltpu.make_async_copy(units.at[slot], parts_hbm.at[unit], y_s.at[unit])
            copy.start()
            y_copies[unit] = copy

    split = 3 * head_cols - 2 * TILE

    def unit_pieces(unit):
        if unit < 3:
            return [(outg_ref.at[:, unit * TILE : (unit + 1) * TILE], 0, TILE)]
        if unit < 6:
            return [(hidg_ref.at[:, (unit - 3) * TILE : (unit - 2) * TILE], 0, TILE)]
        pieces = []
        for part in range(3):
            start = max((unit - 6) * TILE, part * head_cols)
            stop = min((unit - 5) * TILE, (part + 1) * head_cols)
            if start < stop:
                base = part * head_cols
                pieces.append(
                    (
                        qkvg_ref.at[part, :, start - base : stop - base],
                        start - (unit - 6) * TILE,
                        stop - (unit - 6) * TILE,
                    )
                )
        if unit == 8:
            pieces.append((projg_ref, split, TILE))
        return pieces

    def unit_near(unit):
        slot = unit % SLOTS
        first, second = unit_bits(unit)
        mine, other = bits[first], 1 - bits[second]
        got(ry.at[unit], "y", unit, unit_peer(first))
        units[slot, mine, other] = (
            units[slot, mine, other].astype(F32) + ry[unit, other].astype(F32)
        ).astype(BF16)
        z_copies[unit].append(
            send(
                units.at[slot, mine, other], rz.at[unit, 0:2], "z", (unit, 0),
                unit_peer(second),
            )
        )

    def unit_far(unit):
        slot = unit % SLOTS
        first, second = unit_bits(unit)
        mine, same, last = bits[first], bits[second], bits[2]
        got(rz.at[unit, 0:2], "z", (unit, 0), unit_peer(second))

        def summed(which):
            return (
                units[slot, mine, same, which].astype(F32)
                + ry[unit, same, which].astype(F32)
                + rz[unit, which].astype(F32)
            )

        units[slot, mine, same, 1 - last] = summed(1 - last).astype(BF16)
        z_copies[unit].append(
            send(
                units.at[slot, mine, same, 1 - last], rz.at[unit, 2], "z", (unit, 1),
                unit_peer(2),
            )
        )
        total = summed(last)
        for ref, start, stop in unit_pieces(unit):
            ref[...] = total[:, start:stop]

    def unit_end(unit):
        got(rz.at[unit, 2], "z", (unit, 1), unit_peer(2))
        total = rz[unit, 2].astype(F32)
        for ref, start, stop in unit_pieces(unit):
            ref[...] = ref[...] + total[:, start:stop]

    def advance(*stages):
        if reduce_here:
            for stage, unit in stages:
                stage(unit)

    near, far_step, end = unit_near, unit_far, unit_end

    put_unit(0, mm(dmt[...], g_act[:, 0:TILE]), slice(None))
    unit_send(0)
    h2t[...] = ag[...].T
    scatter_halves(lambda rows, at: mm_t(du[rows, :], whid[at, :]), 3)
    put_unit(3, mm(h2t[...], du[:, 0:TILE]), slice(None))
    unit_send(3)
    for j in range(1, 3):
        put_unit(j, mm(dmt[...], g_act[:, j * TILE : (j + 1) * TILE]), slice(None))
        unit_send(j)
    for j in range(1, 3):
        put_unit(3 + j, mm(h2t[...], du[:, j * TILE : (j + 1) * TILE]), slice(None))
        unit_send(3 + j)

    def segments(which, values):
        for i in range(IMG_DEV):
            smp[which * IMG_DEV + i : which * IMG_DEV + i + 1, :] = jnp.sum(
                jnp.where(own_image == i, values, 0.0), axis=0, keepdims=True
            )

    smp[24:32, :] = jnp.zeros((8, width), F32)
    own_grad = scatter_end(rsb, rv1, rv2, 3)
    middle_grad = dy_own[...] + norm_pull(
        n2_own[...], inverse_two, own_grad * (1.0 + mod_rows(4, own_image))
    )
    attn_grad = (middle_grad * mod_rows(2, own_image)).astype(BF16)
    ag[own, :] = attn_grad
    gather_start(row_slot(ag), 9)
    dx1_own[...] = middle_grad
    segments(3, own_grad)
    segments(4, own_grad * n2_own[...])
    segments(2, middle_grad * a_own[...])
    smp[24:25, :] = jnp.sum(attn_grad.astype(F32), axis=0, keepdims=True)
    smp[25:26, :] = jnp.sum(
        (dy_own[...] * mod_rows(5, own_image)).astype(BF16).astype(F32), axis=0, keepdims=True
    )

    def branch_two(j, carry):
        store_blocks(msb, tile(j), mm(g_act[...], wout[:, tile(j)]))
        return carry

    lax.fori_loop(0, width // TILE, branch_two, 0)
    scatter_start(msb, mv1, 6)
    advance((near, 0), (near, 3))
    gather_pass(row_slot(ag), 9)
    scatter_pass(msb, mv1, md2, mv2, 6)
    advance((near, 1), (far_step, 0))
    gather_end(row_slot(ag), 9)

    def back_heads(b, carry):
        at = pl.ds(pl.multiple_of(b * PART, PART), PART)
        rows = mm_t(ag[at, :], wproj[...]).astype(BF16)
        for hd in range(heads):
            doh[hd, at, :] = rows[:, hd * HEAD_DIM : (hd + 1) * HEAD_DIM]
        return carry

    lax.fori_loop(0, 4, back_heads, 0)
    dsb[0:ROWS, :] = jnp.zeros((ROWS, ROWS), BF16)

    def attend_back(hd, carry):
        for at, keys in windows:
            probs = pbs[hd, at, keys].astype(F32)
            prob_grad = mm_t(doh[hd, at, :], qkvh[2 * heads + hd, keys, :])
            row_dot = jnp.sum(probs * prob_grad, axis=1, keepdims=True)
            score_grad = (probs * (prob_grad - row_dot)).astype(BF16)
            dsb[at, keys] = score_grad
            oh[hd, at, :] = (mm(score_grad, qkvh[heads + hd, keys, :]) * scale).astype(BF16)
        qkvh[heads + hd] = (t_mm(qkvh[hd], dsb[0:ROWS, :]) * scale).T.astype(BF16)
        qkvh[2 * heads + hd] = t_mm(doh[hd], pbs[hd]).T.astype(BF16)
        return carry

    lax.fori_loop(0, heads // 2, attend_back, 0)
    advance((near, 2), (far_step, 1))
    lax.fori_loop(heads // 2, heads, attend_back, 0)
    advance((far_step, 2), (end, 0))
    for i in range(3 * heads):
        dqkv[:, i * HEAD_DIM : (i + 1) * HEAD_DIM] = oh[i] if i < heads else qkvh[i]
    finish_sends()

    scatter_halves(lambda rows, at: mm(dqkv[rows, :], wqkv[:, at]), 9)
    h2t[...] = ag[...].T
    advance((near, 4), (end, 1))

    mlp_out = scatter_end(msb, mv1, mv2, 6) + modf[25:26, :]
    segments(5, dy_own[...] * mlp_out)
    final = (x1_own[...] + mod_rows(5, own_image) * mlp_out).astype(BF16)

    def columns_start(rows, base, which):
        for d in range(4):
            fin_out[which, d] = rows[:, d * cols : (d + 1) * cols]
        fin_in[which, t] = fin_out[which, t]
        for k in range(1, 4):
            to = (t + k) % 4
            sent.append(
                send(
                    fin_out.at[which, to], fin_in.at[which, t], "fin", base + k - 1,
                    {"tp": to},
                )
            )

    def columns_end(base, which):
        for k in range(1, 4):
            source = (t + 4 - k) % 4
            got(fin_in.at[which, source], "fin", base + k - 1, {"tp": source})
        return jnp.concatenate([fin_in[which, d] for d in range(4)], axis=0).T

    def place_back(rows_t, initial):
        def one(b, carry):
            at = pl.ds(pl.multiple_of(b * 256, 256), 256)
            rank = rank_row[:, at]
            ids = lax.broadcasted_iota(jnp.int32, (ROWS, 256), 0)
            place = jnp.where(rank == ids, 1.0, 0.0).astype(BF16)
            placed = mm(rows_t, place)
            initial[:, at] = jnp.where(rank >= 0, placed, initial[:, at].astype(F32)).astype(
                BF16
            )
            return carry

        lax.fori_loop(0, toks // 256, one, 0)

    columns_start(final, 0, 0)

    for j in range(2):
        unit_free(j)
        put_unit(6 + j, mm(h1t[...], dqkv[:, j * TILE : (j + 1) * TILE]), slice(None))
        unit_send(6 + j)
    advance((far_step, 4), (end, 2))
    qkv_sum = jnp.sum(dqkv[...].astype(F32), axis=0, keepdims=True)
    hid_sum = jnp.sum(du[...].astype(F32), axis=0, keepdims=True)

    own_grad = scatter_end(rsb, rv1, rv2, 9)
    normed_one, inverse_one = norm_rows(x_own[...].astype(F32))
    segments(0, own_grad)
    segments(1, own_grad * normed_one)
    for d in range(4):
        sms[d] = smp[:, d * cols : (d + 1) * cols]
    for k in range(1, 4):
        to = (t + k) % 4
        sent.append(send(sms.at[to], smr.at[t], "sm", k - 1, {"tp": to}))
    in_grad = dx1_own[...] + norm_pull(
        normed_one, inverse_one, own_grad * (1.0 + mod_rows(1, own_image))
    )
    columns_start(in_grad.astype(BF16), 3, 1)
    advance((near, 5), (far_step, 3))
    total = sms[t]
    for k in range(1, 4):
        source = (t + 4 - k) % 4
        got(smr.at[source], "sm", k - 1, {"tp": source})
        total += smr[source]
    sgr[seq] = total
    sgr[seq, 26:27, :] = qkv_sum[:, 0:head_cols]
    sgr[seq, 27:28, :] = qkv_sum[:, 2 * head_cols : 3 * head_cols]
    for d in range(4):
        sgr[seq, 28 + d : 29 + d, :] = hid_sum[:, d * cols : (d + 1) * cols]

    def tell(k, carry):
        pltpu.make_async_remote_copy(
            src_ref=sgr.at[seq], dst_ref=sgr.at[seq],
            send_sem=sg_s.at[k], recv_sem=sg_r.at[k],
            device_id={"seq": (seq + k) % n_seq}, device_id_type=MESH,
        ).start()
        return carry

    lax.fori_loop(1, n_seq, tell, 0)
    unit_free(2)
    put_unit(8, mm(h1t[...], dqkv[:, 2 * TILE :]), slice(0, split))
    put_unit(8, mm(h2t[...], oc[...]), slice(split, TILE))
    unit_send(8)
    ada_copies = ada_loads()
    advance((far_step, 5), (end, 4))
    place_back(columns_end(0, 0), tok)
    out_copy = pltpu.make_async_copy(tok, output_hbm, out_sem.at[0])
    out_copy.start()
    advance((near, 7))
    advance((near, 6), (end, 5), (end, 3))

    def hear(k, carry):
        source = (seq + n_seq - k) % n_seq
        copy = pltpu.make_async_remote_copy(
            src_ref=sgr.at[seq], dst_ref=sgr.at[source],
            send_sem=sg_s.at[k], recv_sem=sg_r.at[k],
            device_id={"seq": (seq + k) % n_seq}, device_id_type=MESH,
        )
        copy.wait_recv()
        copy.wait_send()
        return carry

    lax.fori_loop(1, n_seq, hear, 0)

    all_rows = n_seq * 32
    flat = parts_of(sgr[...].reshape(all_rows, cols), 2)
    row_id = lax.broadcasted_iota(jnp.int32, (all_rows, images), 0)
    image_id = lax.broadcasted_iota(jnp.int32, (all_rows, images), 1)
    base_image = (row_id >> 5) * IMG_DEV
    place_in = row_id & 31
    act_twice = jnp.concatenate([act_cols[...], act_cols[...]], axis=0)
    cond_part = jnp.zeros((2 * images, width), F32)
    for j in range(6):
        rank_in = place_in - j * IMG_DEV
        member = jnp.where(
            (rank_in >= 0) & (rank_in < IMG_DEV) & (image_id == base_image + rank_in), 1.0, 0.0
        ).astype(BF16)
        found = [t_mm(member, part) for part in flat]
        stacked = jnp.concatenate(found, axis=0).astype(BF16)
        adag_ref[j] = t_mm(act_twice, stacked)
        adabg_ref[j : j + 1, :] = jnp.sum(sum(found), axis=0, keepdims=True)
        ada_copies[j].wait()
        cond_part += mm(stacked, ada_spots[j][...])
        if j == 2:
            advance((far_step, 6))
    cond_part = cond_part[0:images] + cond_part[images:]
    cgr[t] = sum(mm(item, slice_sel[...]) for item in parts_of(cond_part, 2))
    for k in range(1, 4):
        to = (t + k) % 4
        sent.append(send(cgr.at[t], cgr.at[t], "cg", k - 1, {"tp": to}))
    sums = jnp.sum(sgr[:, 24:32, :], axis=0)
    projbg_ref[...] = sums[0:1]
    outbg_ref[...] = sums[1:2]
    qvg_ref[...] = sums[2:4]
    for d in range(4):
        hidbg_ref[:, d * cols : (d + 1) * cols] = sums[4 + d : 5 + d]
    advance((near, 8))
    place_back(columns_end(3, 1), dyt)
    grad_copy = pltpu.make_async_copy(dyt, tokens_grad_hbm, out_sem.at[1])
    grad_copy.start()
    grads = cgr[t]
    for k in range(1, 4):
        source = (t + 4 - k) % 4
        got(cgr.at[source], "cg", k - 1, {"tp": source})
        grads += cgr[source]
    classg_ref[...] = sum(
        lax.dot_general(
            item, label_hot[...], (((0,), (1,)), ((), ())), preferred_element_type=F32
        )
        for item in parts_of(slope_cols[...] * grads, 2)
    )
    advance((end, 6), (far_step, 7), (far_step, 8), (end, 7), (end, 8))
    finish_sends()
    for unit in range(3, UNITS):
        unit_free(unit)
    out_copy.wait()
    grad_copy.wait()


def run_block(sizes, *operands):
    n_seq, width, cols, head_cols, ff, toks, images, classes = sizes
    heads = head_cols // HEAD_DIM
    reduce_here = n_seq == BLOCKS
    step = width // BLOCKS
    slice_width = width // n_seq
    vmem, dma = pltpu.VMEM, pltpu.SemaphoreType.DMA
    any_spec = pl.BlockSpec(memory_space=pl.ANY)
    vmem_spec = pl.BlockSpec(memory_space=pltpu.VMEM)

    def shaped(*shape):
        return jax.ShapeDtypeStruct(shape, F32)

    out_shape = [
        jax.ShapeDtypeStruct((cols, toks), BF16),
        jax.ShapeDtypeStruct((cols, toks), BF16),
        shaped(slice_width, classes),
        shaped(6, slice_width, cols),
        shaped(6, cols),
        shaped(2, cols),
        shaped(1, cols),
        shaped(1, cols),
        shaped(1, ff),
    ]
    out_specs = [any_spec, any_spec] + [vmem_spec] * 7
    if reduce_here:
        out_shape += [
            shaped(3, step, head_cols),
            shaped(step, head_cols),
            shaped(step, ff),
            shaped(step, ff),
        ]
        out_specs += [vmem_spec] * 4
    else:
        out_shape.append(jax.ShapeDtypeStruct((UNITS, 2, 2, 2, step, TILE), BF16))
        out_specs.append(any_spec)
    own = vmem((PART, width), F32)
    low = vmem((ROWS, width), BF16)
    high = vmem((width, ROWS), BF16)
    scratch = [
        vmem((cols, toks), BF16), vmem((cols, toks), BF16),
        vmem((3 * head_cols, width), BF16), vmem((head_cols, width), BF16),
        vmem((width, ff), BF16), vmem((ff, width), BF16), vmem((1, toks), jnp.int32),
        vmem((1, ROWS), jnp.int32),
        high, high,
        vmem((32, width), F32), low, high,
        vmem((3 * heads, ROWS, HEAD_DIM), BF16), vmem((heads, ROWS, ROWS), BF16),
        vmem((heads, ROWS, HEAD_DIM), BF16), vmem((ROWS, head_cols), BF16),
        vmem((2, 2, PART, width), BF16), vmem((2, PART, width), BF16),
        vmem((PART, width), BF16), vmem((PART, width), BF16),
        vmem((2, 2, PART, width), BF16), vmem((2, PART, width), BF16),
        vmem((PART, width), BF16), vmem((PART, width), BF16),
        low, high, low, high, vmem((ROWS, ff), BF16),
        vmem((heads, ROWS, HEAD_DIM), BF16), vmem((ROWS, 3 * head_cols), BF16),
        vmem((SLOTS, 2, 2, 2, step, TILE), BF16),
        vmem((UNITS if reduce_here else 1, 2, 2, step, TILE), BF16),
        vmem((UNITS if reduce_here else 1, BLOCKS // 2 - 1, step, TILE), BF16),
        vmem((2, 4, PART, cols), BF16), vmem((2, 4, PART, cols), BF16),
        vmem((PART, width), BF16), own, own, own, own, own,
        vmem((32, width), F32), vmem((4, 32, cols), F32), vmem((4, 32, cols), F32),
        vmem((4, 32, cols), F32), vmem((n_seq, 32, cols), F32),
        vmem((4, images, slice_width), F32), vmem((width, slice_width), BF16),
        vmem((images, slice_width), F32), vmem((images, slice_width), BF16),
        vmem((classes, images), BF16),
        dma((6,)), dma((6,)), dma((2,)),
        dma((12,)), dma((12,)), dma((12,)), dma((12,)), dma((3,)), dma((3,)),
        dma((6,)), dma((6,)), dma((3,)), dma((3,)), dma((3,)), dma((3,)),
        dma((n_seq,)), dma((n_seq,)),
        dma((UNITS,)), dma((UNITS,)), dma((UNITS, BLOCKS // 2 - 1)), dma((UNITS, BLOCKS // 2 - 1)),
    ]
    return pl.pallas_call(
        functools.partial(block_kernel, sizes),
        out_shape=out_shape,
        in_specs=[pl.BlockSpec(memory_space=pltpu.SMEM)] + [vmem_spec] * 6 + [any_spec] * 7,
        out_specs=out_specs,
        scratch_shapes=scratch,
        compiler_params=pltpu.CompilerParams(
            collective_id=0, has_side_effects=True, vmem_limit_bytes=63 * 1024 * 1024
        ),
    )(*operands)


def copy_kernel(count, *refs):
    sem = refs[3 * count]
    loads = [
        pltpu.make_async_copy(refs[i], refs[2 * count + i], sem.at[0, i]) for i in range(count)
    ]
    stores = [
        pltpu.make_async_copy(refs[2 * count + i], refs[count + i], sem.at[1, i])
        for i in range(count)
    ]
    for load in loads:
        load.start()
    for load, store in zip(loads, stores):
        load.wait()
        store.start()
    for store in stores:
        store.wait()


def copy_all(arrays):
    count = len(arrays)
    return pl.pallas_call(
        functools.partial(copy_kernel, count),
        out_shape=[jax.ShapeDtypeStruct(item.shape, item.dtype) for item in arrays],
        in_specs=[pl.BlockSpec(memory_space=pl.ANY)] * count,
        out_specs=[pl.BlockSpec(memory_space=pl.ANY)] * count,
        scratch_shapes=[pltpu.VMEM(item.shape, item.dtype) for item in arrays]
        + [pltpu.SemaphoreType.DMA((2, count))],
        compiler_params=pltpu.CompilerParams(vmem_limit_bytes=60 * 1024 * 1024),
    )(*arrays)


def time_embed(step_ids, model_width):
    half_width = model_width // 2
    frequency = jnp.exp(-math.log(10000.0) * jnp.arange(half_width, dtype=F32) / half_width)
    angles = step_ids.astype(F32)[:, None] * frequency[None, :]
    return jnp.concatenate([jnp.cos(angles), jnp.sin(angles)], axis=1)


def local(
    tokens,
    out_grad,
    route_mask,
    kept_counts,
    labels,
    timesteps,
    class_table,
    ada_weight,
    ada_bias,
    qkv_weight,
    qv_bias,
    proj_weight,
    proj_bias,
    hidden_weight,
    hidden_bias,
    output_weight,
    output_bias,
):
    n_seq = lax.axis_size("seq")
    toks, cols = tokens.shape
    classes, width = class_table.shape
    head_cols = qkv_weight.shape[2]
    ff = hidden_weight.shape[1]
    images = kept_counts.shape[0]

    label_hot = (labels[:, None] == jnp.arange(classes, dtype=jnp.int32)[None, :]).astype(BF16)
    condition = mm(label_hot, class_table) + time_embed(timesteps, width)
    biases = jnp.concatenate([proj_bias, output_bias, hidden_bias]).astype(F32)

    results = run_block(
        (n_seq, width, cols, head_cols, ff, toks, images, classes),
        kept_counts,
        route_mask.reshape(toks // 128, 128),
        condition,
        labels[None],
        ada_bias,
        qv_bias,
        biases.reshape(-1, cols),
        tokens.T,
        out_grad.T,
        ada_weight.transpose(1, 2, 0).reshape(6 * cols, width),
        qkv_weight.transpose(1, 2, 0).reshape(3 * head_cols, width),
        proj_weight,
        hidden_weight,
        output_weight,
    )
    results = list(copy_all(results if n_seq == BLOCKS else results[:9])) + list(results[9:])
    (
        output,
        tokens_grad,
        class_grad,
        ada_weight_grad,
        ada_bias_grad,
        qv_bias_grad,
        proj_bias_grad,
        output_bias_grad,
        hidden_bias_grad,
    ) = results[:9]
    if n_seq == BLOCKS:
        qkv_weight_grad, proj_weight_grad, hidden_weight_grad, output_weight_grad = results[9:13]
        qkv_weight_grad = qkv_weight_grad.transpose(1, 0, 2)
    else:
        parts = results[9].transpose(3, 2, 1, 4, 0, 5).reshape(width, UNITS * TILE)
        summed = lax.psum_scatter(parts, "seq", scatter_dimension=0, tiled=True).astype(F32)
        output_weight_grad = summed[:, :ff]
        hidden_weight_grad = summed[:, ff : 2 * ff]
        qkv_weight_grad = summed[:, 2 * ff : 2 * ff + 3 * head_cols].reshape(-1, 3, head_cols)
        proj_weight_grad = summed[:, 2 * ff + 3 * head_cols :]
    return (
        output.T,
        tokens_grad.T,
        class_grad.T,
        ada_weight_grad.transpose(1, 0, 2),
        ada_bias_grad,
        qkv_weight_grad,
        qv_bias_grad,
        proj_weight_grad.T,
        proj_bias_grad.reshape(cols),
        hidden_weight_grad,
        hidden_bias_grad.reshape(ff),
        output_weight_grad.T,
        output_bias_grad.reshape(cols),
    )


def solution(mesh):
    return jax.shard_map(
        local,
        mesh=mesh,
        in_specs=(
            P("seq", "tp"),
            P("seq", "tp"),
            P("seq"),
            P(),
            P(),
            P(),
            P(),
            P(None, None, "tp"),
            P(None, "tp"),
            P(None, None, "tp"),
            P(None, "tp"),
            P("tp", None),
            P("tp"),
            P(None, "tp"),
            P("tp"),
            P("tp", None),
            P("tp"),
        ),
        out_specs=(
            P("seq", "tp"),
            P("seq", "tp"),
            P(None, "seq"),
            P("seq", None, "tp"),
            P(None, "tp"),
            P("seq", None, "tp"),
            P(None, "tp"),
            P("tp", "seq"),
            P("tp"),
            P("seq", "tp"),
            P("tp"),
            P("tp", "seq"),
            P("tp"),
        ),
        check_vma=False,
    )
```

```python
import functools
import math

import jax
import jax.numpy as jnp
from jax import lax
from jax.experimental import pallas as pl
from jax.experimental.pallas import tpu as pltpu
from jax.sharding import PartitionSpec as P

HEAD_DIM = 72
IMG_DEV = 4
KEEP_MOST = 192
ROWS = 640
PART = 160
TILE = 384
UNITS = 9
SLOTS = 6
Z_FIRST = (3,)
BLOCKS = 8
NORM_EPS = 1e-06
HIGHEST = lax.Precision.HIGHEST
MESH = pl.DeviceIdType.MESH
F32 = jnp.float32
BF16 = jnp.bfloat16


def mm(left, right):
    return jnp.dot(left, right, preferred_element_type=F32)


def mm_t(left, right):
    return lax.dot_general(left, right, (((1,), (1,)), ((), ())), preferred_element_type=F32)


def t_mm(left, right):
    return lax.dot_general(left, right, (((0,), (0,)), ((), ())), preferred_element_type=F32)


def parts_of(values, count):
    parts = []
    for _ in range(count):
        part = values.astype(BF16)
        parts.append(part)
        values = values - part.astype(F32)
    return parts


def norm_rows(values):
    centered = values - jnp.mean(values, axis=1, keepdims=True)
    inverse = lax.rsqrt(jnp.mean(centered * centered, axis=1, keepdims=True) + NORM_EPS)
    return centered * inverse, inverse


def norm_pull(normed, inverse, grad):
    return inverse * (
        grad
        - jnp.mean(grad, axis=1, keepdims=True)
        - normed * jnp.mean(grad * normed, axis=1, keepdims=True)
    )


def gelu_pair(values):
    coef = math.sqrt(2.0 / math.pi)
    square = values * values
    tanh = jnp.tanh(coef * (values + 0.044715 * (values * square)))
    half = 0.5 * (1.0 + tanh)
    slope = half + 0.5 * values * (1.0 - tanh * tanh) * (
        coef * (1.0 + (3.0 * 0.044715) * square)
    )
    return values * half, slope


def block_kernel(
    sizes,
    counts_ref,
    mask_ref,
    cond_ref,
    labels_ref,
    ada_bias_ref,
    qv_bias_ref,
    bias_ref,
    tokens_hbm,
    grad_hbm,
    ada_hbm,
    wqkv_hbm,
    wproj_hbm,
    whid_hbm,
    wout_hbm,
    output_hbm,
    tokens_grad_hbm,
    classg_ref,
    adag_ref,
    adabg_ref,
    qvg_ref,
    projbg_ref,
    outbg_ref,
    hidbg_ref,
    *rest,
):
    n_seq, width, cols, head_cols, ff, toks, images, classes = sizes
    reduce_here = n_seq == BLOCKS
    slice_width = width // n_seq
    if reduce_here:
        qkvg_ref, projg_ref, hidg_ref, outg_ref = rest[:4]
        rest = rest[4:]
    else:
        parts_hbm = rest[0]
        rest = rest[1:]
    (
        tok, dyt, wqkv, wproj, whid, wout, rank_row, image_lane,
        xg, dyg, modf, h1, h1t, qkvh, pbs, oh, oc, rsb, rv1, sd2, rv2,
        msb, mv1, md2, mv2, ag, h2t, dm, dmt, du, doh, dqkv,
        units, ry, rz, fin_in, fin_out, x_own, a_own, x1_own, n2_own, dx1_own, dy_own,
        smp, sms, smr, modr, sgr, cgr, slice_sel, slope_cols, act_cols, label_hot,
        in_sem, ada_sem, out_sem,
        ag_s, ag_r, rs_s, rs_r, mod_s, mod_r, fin_s, fin_r, sm_s, sm_r, cg_s, cg_r, sg_s, sg_r,
        y_s, y_r, z_s, z_r,
    ) = rest
    heads = head_cols // HEAD_DIM
    scale = HEAD_DIM ** (-0.5)
    g_act = h1
    x_nat = h1
    dy_nat = dm
    dsb = dmt

    seq = lax.axis_index("seq")
    t = lax.axis_index("tp")
    h, l = t // 2, t % 2
    bits = (seq % 2, (seq // 2) % 2, (seq // 4) % 2)
    sib = t + 1 - 2 * l
    far = t + 2 - 4 * h
    diag = 3 - t

    sems = {
        "ag": (ag_s, ag_r), "rs": (rs_s, rs_r), "mod": (mod_s, mod_r), "fin": (fin_s, fin_r),
        "sm": (sm_s, sm_r), "y": (y_s, y_r), "z": (z_s, z_r), "cg": (cg_s, cg_r),
    }

    def remote(src, dst, kind, index, where):
        ssem, rsem = sems[kind]
        return pltpu.make_async_remote_copy(
            src_ref=src, dst_ref=dst, send_sem=ssem.at[index], recv_sem=rsem.at[index],
            device_id=where, device_id_type=MESH,
        )

    def send(src, dst, kind, index, where):
        copy = remote(src, dst, kind, index, where)
        copy.start()
        return copy

    def got(dst, kind, index, where):
        remote(dst, dst, kind, index, where).wait_recv()

    sent = []
    y_copies = {}
    z_copies = {}

    def finish_sends():
        for copy in sent:
            copy.wait_send()
        sent.clear()

    barrier = pltpu.get_barrier_semaphore()
    for k in range(1, 4):
        pl.semaphore_signal(
            barrier, inc=1, device_id={"tp": (t + k) % 4}, device_id_type=MESH
        )

    def greet(k, carry):
        pl.semaphore_signal(
            barrier, inc=1, device_id={"seq": (seq + k) % n_seq}, device_id_type=MESH
        )
        return carry

    lax.fori_loop(1, n_seq, greet, 0)

    ada_spots = [
        buf.at[pl.ds(part * cols, cols)] for buf in (dm, du, h1) for part in range(2)
    ]

    def ada_loads():
        copies = [
            pltpu.make_async_copy(
                ada_hbm.at[pl.ds(j * cols, cols)], ada_spots[j], ada_sem.at[j]
            )
            for j in range(6)
        ]
        for copy in copies:
            copy.start()
        return copies

    loads = [
        pltpu.make_async_copy(src, dst, in_sem.at[i])
        for i, (src, dst) in enumerate(
            [
                (tokens_hbm, tok), (grad_hbm, dyt), (wqkv_hbm, wqkv),
                (wproj_hbm, wproj), (whid_hbm, whid), (wout_hbm, wout),
            ]
        )
    ]
    loads[0].start()
    loads[1].start()
    ada_copies = ada_loads()
    for load in loads[2:]:
        load.start()

    ends = []
    for i in range(IMG_DEV):
        count = counts_ref[seq * IMG_DEV + i]
        ends.append(count if i == 0 else ends[-1] + count)

    def rows_image(start, count):
        ids = lax.broadcasted_iota(jnp.int32, (count, 1), 0) + start
        image = jnp.zeros((count, 1), jnp.int32)
        for i in range(IMG_DEV):
            image += (ids >= ends[i]).astype(jnp.int32)
        return image

    def mod_rows(which, image):
        out = jnp.zeros((image.shape[0], width), F32)
        for i in range(IMG_DEV):
            row = modf[pl.ds(which * IMG_DEV + i, 1), :]
            out = jnp.where(image == i, row, out)
        return out

    mask = mask_ref[...].astype(F32)
    upper = jnp.where(
        lax.broadcasted_iota(jnp.int32, (128, 128), 0)
        <= lax.broadcasted_iota(jnp.int32, (128, 128), 1),
        1.0,
        0.0,
    ).astype(BF16)
    within = mm(mask.astype(BF16), upper)
    before = jnp.zeros((1, 1), F32)
    for i in range(toks // 128):
        row = within[i : i + 1, :]
        rank_row[:, i * 128 : (i + 1) * 128] = jnp.where(
            mask[i : i + 1, :] > 0.0, row + before - 1.0, -1.0
        ).astype(jnp.int32)
        before = before + row[:, 127:128]

    own_cols = pl.ds(pl.multiple_of(t * cols, 32), cols)

    def pick(source, target):
        def one(b, carry):
            ids = lax.broadcasted_iota(jnp.int32, (128, toks), 0) + b * 128
            place = jnp.where(rank_row[...] == ids, 1.0, 0.0).astype(BF16)
            at = pl.ds(pl.multiple_of(b * 128, 128), 128)
            target[own_cols, at] = mm_t(source[...], place).astype(BF16)
            return carry

        lax.fori_loop(0, ROWS // 128, one, 0)

    loads[0].wait()
    pick(tok, xg)

    pl.semaphore_wait(barrier, 3 + n_seq - 1)

    def col_slot(buf):
        return lambda d: buf.at[pl.ds(pl.multiple_of(d * cols, 32), cols)]

    def row_slot(buf):
        return lambda d: buf.at[pl.ds(pl.multiple_of(d * PART, PART), PART)]

    def gather_start(slot, base):
        sent.append(send(slot(t), slot(t), "ag", base, {"tp": far}))
        sent.append(send(slot(t), slot(t), "ag", base + 1, {"tp": sib}))

    def gather_pass(slot, base):
        got(slot(far), "ag", base, {"tp": far})
        sent.append(send(slot(far), slot(far), "ag", base + 2, {"tp": sib}))

    def gather_near(slot, base):
        got(slot(sib), "ag", base + 1, {"tp": sib})

    def gather_last(slot, base):
        got(slot(diag), "ag", base + 2, {"tp": sib})

    def gather_end(slot, base):
        gather_near(slot, base)
        gather_last(slot, base)

    gather_start(col_slot(xg), 0)
    loads[1].wait()
    pick(dyt, dyg)
    act_all = jax.nn.silu(cond_ref[...]).astype(BF16)
    pick_images = jnp.where(
        lax.broadcasted_iota(jnp.int32, (8, images), 1)
        == lax.broadcasted_iota(jnp.int32, (8, images), 0) + seq * IMG_DEV,
        1.0,
        0.0,
    ).astype(BF16)
    act_own = mm(pick_images, act_all).astype(BF16)
    modr[t, 24:32, :] = jnp.zeros((8, cols), F32)
    ada_bias = ada_bias_ref[...].astype(F32)
    qv_bias = qv_bias_ref[...].astype(F32)
    modr[t, 24:25, :] = bias_ref[0:1, :]
    modr[t, 25:26, :] = bias_ref[1:2, :]
    for j in range(6):
        ada_copies[j].wait()
        vectors = mm_t(act_own, ada_spots[j][...]) + ada_bias[j : j + 1]
        modr[t, j * IMG_DEV : (j + 1) * IMG_DEV, :] = vectors[0:IMG_DEV]
    for k in range(1, 4):
        to = (t + k) % 4
        sent.append(send(modr.at[t], modr.at[t], "mod", k - 1, {"tp": to}))
    gather_start(col_slot(dyg), 3)
    gather_pass(col_slot(xg), 0)
    for k in range(1, 4):
        source = (t + 4 - k) % 4
        got(modr.at[source], "mod", k - 1, {"tp": source})
    for d in range(4):
        modf[:, d * cols : (d + 1) * cols] = modr[d]
    gather_end(col_slot(xg), 0)
    x_nat[...] = xg[...].T
    own = pl.ds(pl.multiple_of(t * PART, PART), PART)
    own_image = rows_image(t * PART, PART)
    x_own[...] = x_nat[own, :]

    def norm_one(b, carry):
        at = pl.ds(pl.multiple_of(b * PART, PART), PART)
        image = rows_image(b * PART, PART)
        normed, _ = norm_rows(x_nat[at, :].astype(F32))
        h1[at, :] = (normed * (1.0 + mod_rows(1, image)) + mod_rows(0, image)).astype(BF16)
        return carry

    lax.fori_loop(0, 4, norm_one, 0)
    gather_pass(col_slot(dyg), 3)

    loads[2].wait()
    qkv_bias = jnp.concatenate(
        [qv_bias[0:1], jnp.zeros((1, head_cols), F32), qv_bias[1:2]], axis=1
    )

    def project(b, carry):
        at = pl.ds(pl.multiple_of(b * 320, 320), 320)
        rows = (mm_t(h1[at, :], wqkv[...]) + qkv_bias).astype(BF16)
        for i in range(3 * heads):
            qkvh[i, at, :] = rows[:, i * HEAD_DIM : (i + 1) * HEAD_DIM]
        return carry

    lax.fori_loop(0, 2, project, 0)

    image_row = jnp.zeros((1, ROWS), jnp.int32)
    row_ids = lax.broadcasted_iota(jnp.int32, (1, ROWS), 1)
    for i in range(IMG_DEV):
        image_row += (row_ids >= ends[i]).astype(jnp.int32)

    windows = []
    for b in range(4):
        first = max(0, (b * PART - KEEP_MOST + 1) // 128 * 128)
        last = min(ROWS, -(-((b + 1) * PART + KEEP_MOST - 1) // 128) * 128)
        windows.append((slice(b * PART, (b + 1) * PART), slice(first, last)))

    image_lane[...] = image_row

    def attend_block(b):
        at = pl.ds(pl.multiple_of(b * PART, PART), PART)
        span = 512
        upper_half = b // 2
        keys = pl.ds(pl.multiple_of(upper_half * (ROWS - span), 128), span)
        unused = pl.ds(pl.multiple_of((1 - upper_half) * span, 128), ROWS - span)

        def one(hd, carry):
            scores = mm_t(qkvh[hd, at, :], qkvh[heads + hd, keys, :]) * scale
            masked = jnp.where(
                rows_image(b * PART, PART) == image_lane[:, keys], scores, -1e30
            )
            exps = jnp.exp(masked - jnp.max(masked, axis=1, keepdims=True))
            probs = (exps * (1.0 / jnp.sum(exps, axis=1, keepdims=True))).astype(BF16)
            pbs[hd, at, keys] = probs
            pbs[hd, at, unused] = jnp.zeros((PART, ROWS - span), BF16)
            oh[hd, at, :] = mm(probs, qkvh[2 * heads + hd, keys, :]).astype(BF16)
            return carry

        lax.fori_loop(0, heads, one, 0)
        for hd in range(heads):
            oc[at, hd * HEAD_DIM : (hd + 1) * HEAD_DIM] = oh[hd, at, :]
        rsb[b % 2, b // 2] = mm(oc[at, :], wproj[...]).astype(BF16)

    def store_blocks(buf, tile_at, values):
        low = values.astype(BF16)
        for b in range(4):
            buf[b % 2, b // 2, :, tile_at] = low[b * PART : (b + 1) * PART]

    def scatter_first(buf, first, half, base):
        sent.append(send(buf.at[1 - l, half], first.at[half], "rs", base, {"tp": sib}))

    def scatter_start(buf, first, base):
        scatter_first(buf, first, 1 - h, base)
        scatter_first(buf, first, h, base + 1)

    def scatter_halves(product, base):
        for step, half in ((0, 1 - h), (1, h)):
            rows = pl.ds(pl.multiple_of(half * 2 * PART, 2 * PART), 2 * PART)

            def one(j, carry):
                low = product(rows, tile(j)).astype(BF16)
                for b in range(2):
                    rsb[b, half, :, tile(j)] = low[b * PART : (b + 1) * PART]
                return carry

            lax.fori_loop(0, width // TILE, one, 0)
            scatter_first(rsb, rv1, half, base + step)
            if step == 1:
                scatter_pass(rsb, rv1, sd2, rv2, base)

    def scatter_pass(buf, first, mid, second, base):
        got(first.at[1 - h], "rs", base, {"tp": sib})
        mid[...] = (buf[l, 1 - h].astype(F32) + first[1 - h].astype(F32)).astype(BF16)
        sent.append(send(mid, second, "rs", base + 2, {"tp": far}))

    def scatter_end(buf, first, second, base):
        got(first.at[h], "rs", base + 1, {"tp": sib})
        got(second, "rs", base + 2, {"tp": far})
        return (
            buf[l, h].astype(F32) + first[h].astype(F32) + second[...].astype(F32)
        )

    def tile(j):
        return pl.ds(pl.multiple_of(j * TILE, TILE), TILE)

    loads[3].wait()
    attend_block(diag)
    scatter_first(rsb, rv1, 1 - h, 0)
    attend_block(far)
    scatter_pass(rsb, rv1, sd2, rv2, 0)
    attend_block(sib)
    scatter_first(rsb, rv1, h, 1)
    attend_block(t)
    gather_end(col_slot(dyg), 3)

    dy_nat[...] = dyg[...].T
    dy_own[...] = dy_nat[own, :].astype(F32)

    def out_cotangent(b, carry):
        at = pl.ds(pl.multiple_of(b * PART, PART), PART)
        image = rows_image(b * PART, PART)
        dm[at, :] = (dy_nat[at, :].astype(F32) * mod_rows(5, image)).astype(BF16)
        return carry

    lax.fori_loop(0, 4, out_cotangent, 0)
    h1t[...] = h1[...].T

    attn_out = scatter_end(rsb, rv1, rv2, 0) + modf[24:25, :]
    a_own[...] = attn_out
    middle = x_own[...].astype(F32) + mod_rows(2, own_image) * attn_out
    x1_own[...] = middle
    normed_two, inverse_two = norm_rows(middle.astype(BF16).astype(F32))
    n2_own[...] = normed_two
    ag[own, :] = (normed_two * (1.0 + mod_rows(4, own_image)) + mod_rows(3, own_image)).astype(
        BF16
    )
    gather_start(row_slot(ag), 6)
    own_slice = jnp.where(
        lax.broadcasted_iota(jnp.int32, (width, slice_width), 0)
        == lax.broadcasted_iota(jnp.int32, (width, slice_width), 1) + seq * slice_width,
        1.0,
        0.0,
    ).astype(BF16)
    slice_sel[...] = own_slice
    cond_cols = sum(mm(part, own_slice) for part in parts_of(cond_ref[...], 3))
    sigmoid = jax.nn.sigmoid(cond_cols)
    slope_cols[...] = sigmoid * (1.0 + cond_cols * (1.0 - sigmoid))
    act_cols[...] = mm(jax.nn.silu(cond_ref[...]).astype(BF16), own_slice).astype(BF16)
    label_hot[...] = jnp.where(
        lax.broadcasted_iota(jnp.int32, (classes, images), 0) == labels_ref[...], 1.0, 0.0
    ).astype(BF16)
    dmt[...] = dm[...].T
    loads[4].wait()
    loads[5].wait()
    hidbg_ref[...] = jnp.concatenate([bias_ref[2 + d : 3 + d, :] for d in range(4)], axis=1)

    def mlp(half):
        rows = pl.ds(pl.multiple_of(half * 2 * PART, 2 * PART), 2 * PART)

        def one(j, carry):
            at = tile(j)
            act, slope = gelu_pair(mm(ag[rows, :], whid[:, at]) + hidbg_ref[:, at])
            g_act[rows, at] = act.astype(BF16)
            du[rows, at] = (slope * mm_t(dm[rows, :], wout[at, :])).astype(BF16)
            return carry

        lax.fori_loop(0, ff // TILE, one, 0)

    gather_near(row_slot(ag), 6)
    mlp(h)
    gather_pass(row_slot(ag), 6)
    gather_last(row_slot(ag), 6)
    mlp(1 - h)

    finish_sends()

    def unit_bits(unit):
        return (1, 0) if reduce_here and unit in Z_FIRST else (0, 1)

    def unit_peer(bit):
        return {"seq": seq + (1 - 2 * bits[bit]) * (1 << bit)}

    def put_unit(unit, values, at):
        low = values.astype(BF16)
        step = width // BLOCKS
        first, second = unit_bits(unit)
        for j in range(BLOCKS):
            units[unit % SLOTS, (j >> first) & 1, (j >> second) & 1, j >> 2, :, at] = low[
                j * step : (j + 1) * step
            ]

    def unit_free(unit):
        if reduce_here:
            y_copies.pop(unit).wait_send()
            for copy in z_copies.pop(unit):
                copy.wait_send()
        else:
            y_copies.pop(unit).wait()

    def unit_send(unit):
        slot = unit % SLOTS
        if reduce_here:
            first = unit_bits(unit)[0]
            y_copies[unit] = send(
                units.at[slot, 1 - bits[first]], ry.at[unit], "y", unit, unit_peer(first)
            )
            z_copies[unit] = []
        else:
            copy = pltpu.make_async_copy(units.at[slot], parts_hbm.at[unit], y_s.at[unit])
            copy.start()
            y_copies[unit] = copy

    split = 3 * head_cols - 2 * TILE

    def unit_pieces(unit):
        if unit < 3:
            return [(outg_ref.at[:, unit * TILE : (unit + 1) * TILE], 0, TILE)]
        if unit < 6:
            return [(hidg_ref.at[:, (unit - 3) * TILE : (unit - 2) * TILE], 0, TILE)]
        pieces = []
        for part in range(3):
            start = max((unit - 6) * TILE, part * head_cols)
            stop = min((unit - 5) * TILE, (part + 1) * head_cols)
            if start < stop:
                base = part * head_cols
                pieces.append(
                    (
                        qkvg_ref.at[part, :, start - base : stop - base],
                        start - (unit - 6) * TILE,
                        stop - (unit - 6) * TILE,
                    )
                )
        if unit == 8:
            pieces.append((projg_ref, split, TILE))
        return pieces

    def unit_near(unit):
        slot = unit % SLOTS
        first, second = unit_bits(unit)
        mine, other = bits[first], 1 - bits[second]
        got(ry.at[unit], "y", unit, unit_peer(first))
        units[slot, mine, other] = (
            units[slot, mine, other].astype(F32) + ry[unit, other].astype(F32)
        ).astype(BF16)
        z_copies[unit].append(
            send(
                units.at[slot, mine, other], rz.at[unit, 0:2], "z", (unit, 0),
                unit_peer(second),
            )
        )

    def unit_far(unit):
        slot = unit % SLOTS
        first, second = unit_bits(unit)
        mine, same, last = bits[first], bits[second], bits[2]
        got(rz.at[unit, 0:2], "z", (unit, 0), unit_peer(second))

        def summed(which):
            return (
                units[slot, mine, same, which].astype(F32)
                + ry[unit, same, which].astype(F32)
                + rz[unit, which].astype(F32)
            )

        units[slot, mine, same, 1 - last] = summed(1 - last).astype(BF16)
        z_copies[unit].append(
            send(
                units.at[slot, mine, same, 1 - last], rz.at[unit, 2], "z", (unit, 1),
                unit_peer(2),
            )
        )
        total = summed(last)
        for ref, start, stop in unit_pieces(unit):
            ref[...] = total[:, start:stop]

    def unit_end(unit):
        got(rz.at[unit, 2], "z", (unit, 1), unit_peer(2))
        total = rz[unit, 2].astype(F32)
        for ref, start, stop in unit_pieces(unit):
            ref[...] = ref[...] + total[:, start:stop]

    def advance(*stages):
        if reduce_here:
            for stage, unit in stages:
                stage(unit)

    near, far_step, end = unit_near, unit_far, unit_end

    put_unit(0, mm(dmt[...], g_act[:, 0:TILE]), slice(None))
    unit_send(0)
    h2t[...] = ag[...].T
    scatter_halves(lambda rows, at: mm_t(du[rows, :], whid[at, :]), 3)
    put_unit(3, mm(h2t[...], du[:, 0:TILE]), slice(None))
    unit_send(3)
    for j in range(1, 3):
        put_unit(j, mm(dmt[...], g_act[:, j * TILE : (j + 1) * TILE]), slice(None))
        unit_send(j)
    for j in range(1, 3):
        put_unit(3 + j, mm(h2t[...], du[:, j * TILE : (j + 1) * TILE]), slice(None))
        unit_send(3 + j)

    def segments(which, values):
        for i in range(IMG_DEV):
            smp[which * IMG_DEV + i : which * IMG_DEV + i + 1, :] = jnp.sum(
                jnp.where(own_image == i, values, 0.0), axis=0, keepdims=True
            )

    smp[24:32, :] = jnp.zeros((8, width), F32)
    own_grad = scatter_end(rsb, rv1, rv2, 3)
    middle_grad = dy_own[...] + norm_pull(
        n2_own[...], inverse_two, own_grad * (1.0 + mod_rows(4, own_image))
    )
    attn_grad = (middle_grad * mod_rows(2, own_image)).astype(BF16)
    ag[own, :] = attn_grad
    gather_start(row_slot(ag), 9)
    dx1_own[...] = middle_grad
    segments(3, own_grad)
    segments(4, own_grad * n2_own[...])
    segments(2, middle_grad * a_own[...])
    smp[24:25, :] = jnp.sum(attn_grad.astype(F32), axis=0, keepdims=True)
    smp[25:26, :] = jnp.sum(
        (dy_own[...] * mod_rows(5, own_image)).astype(BF16).astype(F32), axis=0, keepdims=True
    )

    advance((near, 0), (near, 3))

    def branch_two(j, carry):
        store_blocks(msb, tile(j), mm(g_act[...], wout[:, tile(j)]))
        return carry

    lax.fori_loop(0, width // TILE, branch_two, 0)
    scatter_start(msb, mv1, 6)
    gather_pass(row_slot(ag), 9)
    scatter_pass(msb, mv1, md2, mv2, 6)
    advance((near, 1), (far_step, 0))
    gather_end(row_slot(ag), 9)

    def back_heads(b, carry):
        at = pl.ds(pl.multiple_of(b * PART, PART), PART)
        rows = mm_t(ag[at, :], wproj[...]).astype(BF16)
        for hd in range(heads):
            doh[hd, at, :] = rows[:, hd * HEAD_DIM : (hd + 1) * HEAD_DIM]
        return carry

    lax.fori_loop(0, 4, back_heads, 0)
    dsb[0:ROWS, :] = jnp.zeros((ROWS, ROWS), BF16)

    def attend_back(hd, carry):
        for at, keys in windows:
            probs = pbs[hd, at, keys].astype(F32)
            prob_grad = mm_t(doh[hd, at, :], qkvh[2 * heads + hd, keys, :])
            row_dot = jnp.sum(probs * prob_grad, axis=1, keepdims=True)
            score_grad = (probs * (prob_grad - row_dot)).astype(BF16)
            dsb[at, keys] = score_grad
            oh[hd, at, :] = (mm(score_grad, qkvh[heads + hd, keys, :]) * scale).astype(BF16)
        qkvh[heads + hd] = (t_mm(qkvh[hd], dsb[0:ROWS, :]) * scale).T.astype(BF16)
        qkvh[2 * heads + hd] = t_mm(doh[hd], pbs[hd]).T.astype(BF16)
        return carry

    lax.fori_loop(0, heads // 2, attend_back, 0)
    advance((near, 2), (far_step, 1))
    lax.fori_loop(heads // 2, heads, attend_back, 0)
    advance((far_step, 2), (end, 0))
    for i in range(3 * heads):
        dqkv[:, i * HEAD_DIM : (i + 1) * HEAD_DIM] = oh[i] if i < heads else qkvh[i]
    finish_sends()

    scatter_halves(lambda rows, at: mm(dqkv[rows, :], wqkv[:, at]), 9)
    h2t[...] = ag[...].T
    advance((near, 4), (end, 1))

    mlp_out = scatter_end(msb, mv1, mv2, 6) + modf[25:26, :]
    segments(5, dy_own[...] * mlp_out)
    final = (x1_own[...] + mod_rows(5, own_image) * mlp_out).astype(BF16)

    def columns_start(rows, base, which):
        for d in range(4):
            fin_out[which, d] = rows[:, d * cols : (d + 1) * cols]
        fin_in[which, t] = fin_out[which, t]
        for k in range(1, 4):
            to = (t + k) % 4
            sent.append(
                send(
                    fin_out.at[which, to], fin_in.at[which, t], "fin", base + k - 1,
                    {"tp": to},
                )
            )

    def columns_end(base, which):
        for k in range(1, 4):
            source = (t + 4 - k) % 4
            got(fin_in.at[which, source], "fin", base + k - 1, {"tp": source})
        return jnp.concatenate([fin_in[which, d] for d in range(4)], axis=0).T

    def place_back(rows_t, initial):
        def one(b, carry):
            at = pl.ds(pl.multiple_of(b * 256, 256), 256)
            rank = rank_row[:, at]
            ids = lax.broadcasted_iota(jnp.int32, (ROWS, 256), 0)
            place = jnp.where(rank == ids, 1.0, 0.0).astype(BF16)
            placed = mm(rows_t, place)
            initial[:, at] = jnp.where(rank >= 0, placed, initial[:, at].astype(F32)).astype(
                BF16
            )
            return carry

        lax.fori_loop(0, toks // 256, one, 0)

    columns_start(final, 0, 0)

    for j in range(2):
        unit_free(j)
        put_unit(6 + j, mm(h1t[...], dqkv[:, j * TILE : (j + 1) * TILE]), slice(None))
        unit_send(6 + j)
    advance((far_step, 4), (end, 2))
    qkv_sum = jnp.sum(dqkv[...].astype(F32), axis=0, keepdims=True)
    hid_sum = jnp.sum(du[...].astype(F32), axis=0, keepdims=True)

    own_grad = scatter_end(rsb, rv1, rv2, 9)
    normed_one, inverse_one = norm_rows(x_own[...].astype(F32))
    segments(0, own_grad)
    segments(1, own_grad * normed_one)
    for d in range(4):
        sms[d] = smp[:, d * cols : (d + 1) * cols]
    for k in range(1, 4):
        to = (t + k) % 4
        sent.append(send(sms.at[to], smr.at[t], "sm", k - 1, {"tp": to}))
    in_grad = dx1_own[...] + norm_pull(
        normed_one, inverse_one, own_grad * (1.0 + mod_rows(1, own_image))
    )
    columns_start(in_grad.astype(BF16), 3, 1)
    advance((near, 5), (far_step, 3))
    total = sms[t]
    for k in range(1, 4):
        source = (t + 4 - k) % 4
        got(smr.at[source], "sm", k - 1, {"tp": source})
        total += smr[source]
    sgr[seq] = total
    sgr[seq, 26:27, :] = qkv_sum[:, 0:head_cols]
    sgr[seq, 27:28, :] = qkv_sum[:, 2 * head_cols : 3 * head_cols]
    for d in range(4):
        sgr[seq, 28 + d : 29 + d, :] = hid_sum[:, d * cols : (d + 1) * cols]

    def tell(k, carry):
        pltpu.make_async_remote_copy(
            src_ref=sgr.at[seq], dst_ref=sgr.at[seq],
            send_sem=sg_s.at[k], recv_sem=sg_r.at[k],
            device_id={"seq": (seq + k) % n_seq}, device_id_type=MESH,
        ).start()
        return carry

    lax.fori_loop(1, n_seq, tell, 0)
    unit_free(2)
    put_unit(8, mm(h1t[...], dqkv[:, 2 * TILE :]), slice(0, split))
    put_unit(8, mm(h2t[...], oc[...]), slice(split, TILE))
    unit_send(8)
    ada_copies = ada_loads()
    advance((far_step, 5), (end, 4))
    place_back(columns_end(0, 0), tok)
    out_copy = pltpu.make_async_copy(tok, output_hbm, out_sem.at[0])
    out_copy.start()
    advance((near, 6),)
    advance((end, 5), (end, 3))

    def hear(k, carry):
        source = (seq + n_seq - k) % n_seq
        copy = pltpu.make_async_remote_copy(
            src_ref=sgr.at[seq], dst_ref=sgr.at[source],
            send_sem=sg_s.at[k], recv_sem=sg_r.at[k],
            device_id={"seq": (seq + k) % n_seq}, device_id_type=MESH,
        )
        copy.wait_recv()
        copy.wait_send()
        return carry

    lax.fori_loop(1, n_seq, hear, 0)

    all_rows = n_seq * 32
    flat = parts_of(sgr[...].reshape(all_rows, cols), 2)
    row_id = lax.broadcasted_iota(jnp.int32, (all_rows, images), 0)
    image_id = lax.broadcasted_iota(jnp.int32, (all_rows, images), 1)
    base_image = (row_id >> 5) * IMG_DEV
    place_in = row_id & 31
    act_twice = jnp.concatenate([act_cols[...], act_cols[...]], axis=0)
    cond_part = jnp.zeros((2 * images, width), F32)
    for j in range(6):
        rank_in = place_in - j * IMG_DEV
        member = jnp.where(
            (rank_in >= 0) & (rank_in < IMG_DEV) & (image_id == base_image + rank_in), 1.0, 0.0
        ).astype(BF16)
        found = [t_mm(member, part) for part in flat]
        stacked = jnp.concatenate(found, axis=0).astype(BF16)
        adag_ref[j] = t_mm(act_twice, stacked)
        adabg_ref[j : j + 1, :] = jnp.sum(sum(found), axis=0, keepdims=True)
        ada_copies[j].wait()
        cond_part += mm(stacked, ada_spots[j][...])
        if j == 2:
            advance((far_step, 6), (near, 7))
    cond_part = cond_part[0:images] + cond_part[images:]
    cgr[t] = sum(mm(item, slice_sel[...]) for item in parts_of(cond_part, 2))
    for k in range(1, 4):
        to = (t + k) % 4
        sent.append(send(cgr.at[t], cgr.at[t], "cg", k - 1, {"tp": to}))
    sums = jnp.sum(sgr[:, 24:32, :], axis=0)
    projbg_ref[...] = sums[0:1]
    outbg_ref[...] = sums[1:2]
    qvg_ref[...] = sums[2:4]
    for d in range(4):
        hidbg_ref[:, d * cols : (d + 1) * cols] = sums[4 + d : 5 + d]
    advance((near, 8),)
    place_back(columns_end(3, 1), dyt)
    grad_copy = pltpu.make_async_copy(dyt, tokens_grad_hbm, out_sem.at[1])
    grad_copy.start()
    grads = cgr[t]
    for k in range(1, 4):
        source = (t + 4 - k) % 4
        got(cgr.at[source], "cg", k - 1, {"tp": source})
        grads += cgr[source]
    classg_ref[...] = sum(
        lax.dot_general(
            item, label_hot[...], (((0,), (1,)), ((), ())), preferred_element_type=F32
        )
        for item in parts_of(slope_cols[...] * grads, 2)
    )
    advance((end, 6), (far_step, 7), (far_step, 8), (end, 7), (end, 8))
    finish_sends()
    for unit in range(3, UNITS):
        unit_free(unit)
    out_copy.wait()
    grad_copy.wait()


def run_block(sizes, *operands):
    n_seq, width, cols, head_cols, ff, toks, images, classes = sizes
    heads = head_cols // HEAD_DIM
    reduce_here = n_seq == BLOCKS
    step = width // BLOCKS
    slice_width = width // n_seq
    vmem, dma = pltpu.VMEM, pltpu.SemaphoreType.DMA
    any_spec = pl.BlockSpec(memory_space=pl.ANY)
    vmem_spec = pl.BlockSpec(memory_space=pltpu.VMEM)

    def shaped(*shape):
        return jax.ShapeDtypeStruct(shape, F32)

    out_shape = [
        jax.ShapeDtypeStruct((cols, toks), BF16),
        jax.ShapeDtypeStruct((cols, toks), BF16),
        shaped(slice_width, classes),
        shaped(6, slice_width, cols),
        shaped(6, cols),
        shaped(2, cols),
        shaped(1, cols),
        shaped(1, cols),
        shaped(1, ff),
    ]
    out_specs = [any_spec, any_spec] + [vmem_spec] * 7
    if reduce_here:
        out_shape += [
            shaped(3, step, head_cols),
            shaped(step, head_cols),
            shaped(step, ff),
            shaped(step, ff),
        ]
        out_specs += [vmem_spec] * 4
    else:
        out_shape.append(jax.ShapeDtypeStruct((UNITS, 2, 2, 2, step, TILE), BF16))
        out_specs.append(any_spec)
    own = vmem((PART, width), F32)
    low = vmem((ROWS, width), BF16)
    high = vmem((width, ROWS), BF16)
    scratch = [
        vmem((cols, toks), BF16), vmem((cols, toks), BF16),
        vmem((3 * head_cols, width), BF16), vmem((head_cols, width), BF16),
        vmem((width, ff), BF16), vmem((ff, width), BF16), vmem((1, toks), jnp.int32),
        vmem((1, ROWS), jnp.int32),
        high, high,
        vmem((32, width), F32), low, high,
        vmem((3 * heads, ROWS, HEAD_DIM), BF16), vmem((heads, ROWS, ROWS), BF16),
        vmem((heads, ROWS, HEAD_DIM), BF16), vmem((ROWS, head_cols), BF16),
        vmem((2, 2, PART, width), BF16), vmem((2, PART, width), BF16),
        vmem((PART, width), BF16), vmem((PART, width), BF16),
        vmem((2, 2, PART, width), BF16), vmem((2, PART, width), BF16),
        vmem((PART, width), BF16), vmem((PART, width), BF16),
        low, high, low, high, vmem((ROWS, ff), BF16),
        vmem((heads, ROWS, HEAD_DIM), BF16), vmem((ROWS, 3 * head_cols), BF16),
        vmem((SLOTS, 2, 2, 2, step, TILE), BF16),
        vmem((UNITS if reduce_here else 1, 2, 2, step, TILE), BF16),
        vmem((UNITS if reduce_here else 1, BLOCKS // 2 - 1, step, TILE), BF16),
        vmem((2, 4, PART, cols), BF16), vmem((2, 4, PART, cols), BF16),
        vmem((PART, width), BF16), own, own, own, own, own,
        vmem((32, width), F32), vmem((4, 32, cols), F32), vmem((4, 32, cols), F32),
        vmem((4, 32, cols), F32), vmem((n_seq, 32, cols), F32),
        vmem((4, images, slice_width), F32), vmem((width, slice_width), BF16),
        vmem((images, slice_width), F32), vmem((images, slice_width), BF16),
        vmem((classes, images), BF16),
        dma((6,)), dma((6,)), dma((2,)),
        dma((12,)), dma((12,)), dma((12,)), dma((12,)), dma((3,)), dma((3,)),
        dma((6,)), dma((6,)), dma((3,)), dma((3,)), dma((3,)), dma((3,)),
        dma((n_seq,)), dma((n_seq,)),
        dma((UNITS,)), dma((UNITS,)), dma((UNITS, BLOCKS // 2 - 1)), dma((UNITS, BLOCKS // 2 - 1)),
    ]
    return pl.pallas_call(
        functools.partial(block_kernel, sizes),
        out_shape=out_shape,
        in_specs=[pl.BlockSpec(memory_space=pltpu.SMEM)] + [vmem_spec] * 6 + [any_spec] * 7,
        out_specs=out_specs,
        scratch_shapes=scratch,
        compiler_params=pltpu.CompilerParams(
            collective_id=0, has_side_effects=True, vmem_limit_bytes=63 * 1024 * 1024
        ),
    )(*operands)


def copy_kernel(count, *refs):
    sem = refs[3 * count]
    loads = [
        pltpu.make_async_copy(refs[i], refs[2 * count + i], sem.at[0, i]) for i in range(count)
    ]
    stores = [
        pltpu.make_async_copy(refs[2 * count + i], refs[count + i], sem.at[1, i])
        for i in range(count)
    ]
    for load in loads:
        load.start()
    for load, store in zip(loads, stores):
        load.wait()
        store.start()
    for store in stores:
        store.wait()


def copy_all(arrays):
    count = len(arrays)
    return pl.pallas_call(
        functools.partial(copy_kernel, count),
        out_shape=[jax.ShapeDtypeStruct(item.shape, item.dtype) for item in arrays],
        in_specs=[pl.BlockSpec(memory_space=pl.ANY)] * count,
        out_specs=[pl.BlockSpec(memory_space=pl.ANY)] * count,
        scratch_shapes=[pltpu.VMEM(item.shape, item.dtype) for item in arrays]
        + [pltpu.SemaphoreType.DMA((2, count))],
        compiler_params=pltpu.CompilerParams(vmem_limit_bytes=60 * 1024 * 1024),
    )(*arrays)


def time_embed(step_ids, model_width):
    half_width = model_width // 2
    frequency = jnp.exp(-math.log(10000.0) * jnp.arange(half_width, dtype=F32) / half_width)
    angles = step_ids.astype(F32)[:, None] * frequency[None, :]
    return jnp.concatenate([jnp.cos(angles), jnp.sin(angles)], axis=1)


def local(
    tokens,
    out_grad,
    route_mask,
    kept_counts,
    labels,
    timesteps,
    class_table,
    ada_weight,
    ada_bias,
    qkv_weight,
    qv_bias,
    proj_weight,
    proj_bias,
    hidden_weight,
    hidden_bias,
    output_weight,
    output_bias,
):
    n_seq = lax.axis_size("seq")
    toks, cols = tokens.shape
    classes, width = class_table.shape
    head_cols = qkv_weight.shape[2]
    ff = hidden_weight.shape[1]
    images = kept_counts.shape[0]

    label_hot = (labels[:, None] == jnp.arange(classes, dtype=jnp.int32)[None, :]).astype(BF16)
    condition = mm(label_hot, class_table) + time_embed(timesteps, width)
    biases = jnp.concatenate([proj_bias, output_bias, hidden_bias]).astype(F32)

    results = run_block(
        (n_seq, width, cols, head_cols, ff, toks, images, classes),
        kept_counts,
        route_mask.reshape(toks // 128, 128),
        condition,
        labels[None],
        ada_bias,
        qv_bias,
        biases.reshape(-1, cols),
        tokens.T,
        out_grad.T,
        ada_weight.transpose(1, 2, 0).reshape(6 * cols, width),
        qkv_weight.transpose(1, 2, 0).reshape(3 * head_cols, width),
        proj_weight,
        hidden_weight,
        output_weight,
    )
    results = list(copy_all(results if n_seq == BLOCKS else results[:9])) + list(results[9:])
    (
        output,
        tokens_grad,
        class_grad,
        ada_weight_grad,
        ada_bias_grad,
        qv_bias_grad,
        proj_bias_grad,
        output_bias_grad,
        hidden_bias_grad,
    ) = results[:9]
    if n_seq == BLOCKS:
        qkv_weight_grad, proj_weight_grad, hidden_weight_grad, output_weight_grad = results[9:13]
        qkv_weight_grad = qkv_weight_grad.transpose(1, 0, 2)
    else:
        parts = results[9].transpose(3, 2, 1, 4, 0, 5).reshape(width, UNITS * TILE)
        summed = lax.psum_scatter(parts, "seq", scatter_dimension=0, tiled=True).astype(F32)
        output_weight_grad = summed[:, :ff]
        hidden_weight_grad = summed[:, ff : 2 * ff]
        qkv_weight_grad = summed[:, 2 * ff : 2 * ff + 3 * head_cols].reshape(-1, 3, head_cols)
        proj_weight_grad = summed[:, 2 * ff + 3 * head_cols :]
    return (
        output.T,
        tokens_grad.T,
        class_grad.T,
        ada_weight_grad.transpose(1, 0, 2),
        ada_bias_grad,
        qkv_weight_grad,
        qv_bias_grad,
        proj_weight_grad.T,
        proj_bias_grad.reshape(cols),
        hidden_weight_grad,
        hidden_bias_grad.reshape(ff),
        output_weight_grad.T,
        output_bias_grad.reshape(cols),
    )


def solution(mesh):
    return jax.shard_map(
        local,
        mesh=mesh,
        in_specs=(
            P("seq", "tp"),
            P("seq", "tp"),
            P("seq"),
            P(),
            P(),
            P(),
            P(),
            P(None, None, "tp"),
            P(None, "tp"),
            P(None, None, "tp"),
            P(None, "tp"),
            P("tp", None),
            P("tp"),
            P(None, "tp"),
            P("tp"),
            P("tp", None),
            P("tp"),
        ),
        out_specs=(
            P("seq", "tp"),
            P("seq", "tp"),
            P(None, "seq"),
            P("seq", None, "tp"),
            P(None, "tp"),
            P("seq", None, "tp"),
            P(None, "tp"),
            P("tp", "seq"),
            P("tp"),
            P("seq", "tp"),
            P("tp"),
            P("tp", "seq"),
            P("tp"),
        ),
        check_vma=False,
    )
```
